32 devices in a mesh: pair: 4 (over x, core), row: 2 (over y), col: 4 (over z).
Axes of the slice: x: 2, y: 2, z: 4, core: 2. Of those that a mesh axis runs over, the one named last changes fastest.
Arguments:
- coords: float32 [4, 30, 512], P('pair', None, ('row', 'col')), may hold values from -1.6 to 1.6
- final_coords: float32 [30, 512], P(None, ('row', 'col')), may hold values from -1.6 to 1.6
- growth: float32 [4, 512], P('pair', ('row', 'col')), may hold values from 0.4 to 2.5
- counts: int32 [5], replicated, may hold values from 256 to 512, as said below
- labels: int32 [512], P(('row', 'col')), may hold values from 0 to 15
Outputs:
- fates: float32 [4, 16, 512], P('pair', None, ('row', 'col'))
- mass: float32 [4, 512], P('pair', ('row', 'col'))
The draws below stay inside these ranges and needn't reach their ends.
Inputs may be any that keep to these rules, and one draw needn't show every extreme that they name: The cells of a timepoint are its first counts positions; some timepoint has all 512.
All inputs are finite; a program needn't handle non-finite values.
Results may differ from the reference program's by a relative error of at most 0.0001.
Values sent between devices are 32-bit elements; how exact they have to be, the bound alone decides.
A program may use at most 64 MiB of HBM per device.

```python
import math
import jax
import jax.numpy as jnp
from jax import lax

PCA = 30
CLASSES = 16
PAIRS = 4
CELLS = 512


def membership(key, moment):
    member_key = jax.random.fold_in(jax.random.fold_in(key, 51), moment)
    return jax.random.randint(member_key, (CELLS,), 0, CLASSES).astype(jnp.int32)


def cloud(key, moment):
    member = membership(key, moment)
    across = (member % 4).astype(jnp.float32) * 0.9 - 1.35
    downward = (member // 4).astype(jnp.float32) * 0.9 - 1.35
    noise_key = jax.random.fold_in(jax.random.fold_in(key, 52), moment)
    near_noise = 0.12 * jax.random.normal(jax.random.fold_in(noise_key, 3), (2, CELLS), jnp.float32)
    far_noise = 0.3 * jax.random.normal(jax.random.fold_in(noise_key, 4), (PCA - 2, CELLS), jnp.float32)
    centers = jnp.stack([across, downward], axis=0)
    values = jnp.concatenate([centers + near_noise, far_noise], axis=0)
    return jnp.clip(values, -1.6, 1.6).astype(jnp.float32)


def draw_coords(key, part):
    return jnp.stack([cloud(key, moment) for moment in range(PAIRS)], axis=0)


def draw_final_coords(key, part):
    return cloud(key, PAIRS)


def draw_labels(key, part):
    return membership(key, PAIRS)


def draw_counts(key, part):
    base = jax.random.randint(jax.random.fold_in(key, 41), (PAIRS + 1,), CELLS // 2, CELLS + 1)
    chosen = jax.random.randint(jax.random.fold_in(key, 42), (), 0, PAIRS + 1)
    return jnp.where(jnp.arange(PAIRS + 1) == chosen, CELLS, base).astype(jnp.int32)


def block_levels(rng, dims, split, least, top_value):
    def one(dim, shards_of):
        heights = jax.random.uniform(jax.random.fold_in(jax.random.fold_in(rng, 6), dim), (shards_of,), jnp.float32, least / len(split), top_value / len(split))
        return jnp.repeat(jnp.exp(heights), dims[dim] // shards_of).reshape((-1,) + (1,) * (len(dims) - dim - 1))

    factor_of = one(*split[0])
    for cut in split[1:]:
        factor_of = factor_of * one(*cut)
    return factor_of


def setup_inputs(seed: int = 0) -> dict:
    seeds = jax.random.split(jax.random.key(seed), 6)
    return {
        "coords": draw_coords(jax.random.fold_in(seeds[5], 71), 0),
        "final_coords": draw_final_coords(jax.random.fold_in(seeds[5], 71), 0),
        "growth": jnp.clip(jnp.exp(math.log(2.5) - 1.8325814 * jax.random.uniform(seeds[2], (PAIRS, CELLS), jnp.float32) ** block_levels(seeds[2], (PAIRS, CELLS), ((0, 4), (1, 8)), -0.2, 0.2)), 0.4, 2.5),
        "counts": draw_counts(jax.random.fold_in(seeds[5], 71), 0),
        "labels": draw_labels(jax.random.fold_in(seeds[5], 71), 0),
    }


cost_scale = 1.0
source_power = 0.5
target_power = 50.0 / 51.0


def kernel_block(source_block, targets, target_norms):
    cross = lax.dot_general(source_block, targets, (((0,), (0,)), ((), ())), precision=lax.Precision.HIGHEST, preferred_element_type=jnp.float32)
    source_norms = jnp.sum(source_block * source_block, axis=0)
    return jnp.exp(-(source_norms[:, None] + target_norms[None, :] - 2.0 * cross) / cost_scale)


def split_rows(sources, width):
    number = sources.shape[1] // width
    return jnp.transpose(sources.reshape(sources.shape[0], number, width), (1, 0, 2))


def forward(blocks, targets, target_norms, weights):
    def block_out(source_block):
        kernel = kernel_block(source_block, targets, target_norms)
        return lax.dot_general(weights, kernel, (((1,), (1,)), ((), ())), precision=lax.Precision.HIGHEST, preferred_element_type=jnp.float32)

    outputs = lax.map(block_out, blocks)
    return jnp.transpose(outputs, (1, 0, 2)).reshape(weights.shape[0], -1)


def backward(blocks, targets, target_norms, scales):
    scale_blocks = scales.reshape(blocks.shape[0], blocks.shape[2])

    def block_in(pieces):
        kernel = kernel_block(pieces[0], targets, target_norms)
        return jnp.dot(pieces[1], kernel, precision=lax.Precision.HIGHEST, preferred_element_type=jnp.float32)

    return jnp.sum(lax.map(block_in, (blocks, scale_blocks)), axis=0)


def reference(coords, final_coords, growth, counts, labels):
    pairs = coords.shape[0]
    cells = coords.shape[2]
    width = min(512, cells)
    index = lax.iota(jnp.int32, cells)
    saved = []
    masses = []
    for pair in range(pairs):
        sources = coords[pair]
        targets = coords[pair + 1] if pair + 1 < pairs else final_coords
        source_valid = index < counts[pair]
        target_valid = index < counts[pair + 1]
        source_total = counts[pair].astype(jnp.float32)
        target_total = counts[pair + 1].astype(jnp.float32)
        blocks = split_rows(sources, width)
        target_norms = jnp.sum(targets * targets, axis=0)
        start_rows = forward(blocks, targets, target_norms, target_valid.astype(jnp.float32)[None, :])[0]
        source_mass = jnp.where(source_valid, growth[pair] / source_total, 0.0)
        scale_u = jnp.where(source_valid, jnp.power(source_mass / start_rows, source_power), 0.0)
        column_totals = backward(blocks, targets, target_norms, scale_u)
        target_mass = target_valid.astype(jnp.float32) / target_total
        scale_v = jnp.where(target_valid, jnp.power(target_mass / column_totals, target_power), 0.0)
        row_totals = forward(blocks, targets, target_norms, scale_v[None, :])[0]
        masses.append(jnp.where(source_valid, source_total * scale_u * row_totals, 0.0))
        saved.append((blocks, targets, target_norms, scale_v, row_totals, source_valid))
    classes = lax.iota(jnp.int32, CLASSES)
    final_valid = index < counts[pairs]
    carried = jnp.where((labels[None, :] == classes[:, None]) & final_valid[None, :], 1.0, 0.0).astype(jnp.float32)
    results = [None] * pairs
    for pair in range(pairs - 1, -1, -1):
        blocks, targets, target_norms, scale_v, row_totals, source_valid = saved[pair]
        terms = forward(blocks, targets, target_norms, carried * scale_v[None, :])
        carried = jnp.where(source_valid[None, :], terms / jnp.where(source_valid, row_totals, 1.0)[None, :], 0.0)
        results[pair] = carried
    return jnp.stack(results), jnp.stack(masses)
```

```python
import functools
import jax
import jax.numpy as jnp
from jax import lax
from jax.experimental import pallas as pl
from jax.experimental.pallas import tpu as pltpu
from jax.sharding import PartitionSpec as P

CLASSES = 16
FUSED_BYTES = 16 * 1024 * 1024


cost_scale = 1.0
source_power = 0.5
target_power = 50.0 / 51.0


def shifted_2(block, axis, distance):
    devices = range(lax.axis_size(axis))
    route = [(i - distance, i) for i in devices if i - distance in devices]
    return lax.ppermute(block, axis, route)


def kernel_tile(sources, targets):
    cross = lax.dot_general(
        sources,
        targets,
        (((0,), (0,)), ((), ())),
        precision=lax.Precision.HIGHEST,
        preferred_element_type=jnp.float32,
    )
    source_norms = jnp.sum(sources * sources, axis=0)
    target_norms = jnp.sum(targets * targets, axis=0)
    return jnp.exp(-(source_norms[:, None] + target_norms[None, :] - 2.0 * cross) / cost_scale)


def forward(kernel, weights):
    return lax.dot_general(
        weights,
        kernel,
        (((1,), (1,)), ((), ())),
        precision=lax.Precision.HIGHEST,
        preferred_element_type=jnp.float32,
    )


def backward(kernel, scales):
    return jnp.dot(
        scales, kernel, precision=lax.Precision.HIGHEST, preferred_element_type=jnp.float32
    )


def per_device(coords, final_coords, growth, counts, labels):
    tile = coords.shape[2]
    n_pair = lax.axis_size("pair")
    n_row = lax.axis_size("row")
    n_col = lax.axis_size("col")
    pair_at = lax.axis_index("pair")
    row_at = lax.axis_index("row")
    col_at = lax.axis_index("col")
    source_count = n_col * tile
    target_count = n_row * tile
    own_coords = coords[0]
    sources, source_growth = (
        lax.all_gather(own_coords, "col", axis=1, tiled=True),
        lax.all_gather(growth[0], "col", axis=0, tiled=True),
    )
    shifted = shifted_2(own_coords, "pair", -1)
    is_last = pair_at == n_pair - 1
    own_targets = jnp.where(is_last, final_coords, shifted)
    label_values = labels.astype(jnp.float32)
    position = lax.iota(jnp.int32, target_count)
    targets, target_labels = (
        lax.all_gather(own_targets, "row", axis=1, tiled=True),
        lax.all_gather(label_values, "row", axis=0, tiled=True),
    )
    target_index = position // tile * (n_col * tile) + col_at * tile + position % tile

    def hand_over(fates_now):
        incoming = shifted_2(fates_now, "pair", -1)
        return lax.all_gather(incoming, "row", axis=1, tiled=True)

    source_number = counts[pair_at]
    target_number = counts[pair_at + 1]
    source_total = source_number.astype(jnp.float32)
    target_total = target_number.astype(jnp.float32)
    source_index = row_at * source_count + lax.iota(jnp.int32, source_count)
    source_valid = source_index < source_number
    target_valid = target_index < target_number
    kernel = kernel_tile(sources, targets)
    start_terms = forward(kernel, target_valid.astype(jnp.float32)[None, :])[0]
    start_rows = lax.psum(start_terms, "col")
    source_mass = jnp.where(source_valid, source_growth / source_total, 0.0)
    scale_u = jnp.where(source_valid, jnp.power(source_mass / start_rows, source_power), 0.0)
    column_terms = backward(kernel, scale_u)
    column_totals = lax.psum(column_terms, "row")
    target_mass = target_valid.astype(jnp.float32) / target_total
    scale_v = jnp.where(target_valid, jnp.power(target_mass / column_totals, target_power), 0.0)
    own_offset = col_at * tile
    own_valid = lax.dynamic_slice_in_dim(source_valid, own_offset, tile, 0)
    own_scale = lax.dynamic_slice_in_dim(scale_u, own_offset, tile, 0)
    class_values = lax.iota(jnp.int32, CLASSES).astype(jnp.float32)
    label_table = jnp.where(
        (target_labels[None, :] == class_values[:, None]) & target_valid[None, :], 1.0, 0.0
    ).astype(jnp.float32)
    empty = jnp.zeros((CLASSES, tile), jnp.float32)
    final_terms = forward(kernel, scale_v[None, :])[0]
    final_rows = lax.psum(final_terms, "col")
    own_rows = lax.dynamic_slice_in_dim(final_rows, own_offset, tile, 0)
    safe_rows = jnp.where(own_valid, own_rows, 1.0)

    def advance(turn, fates_now):
        carried = jnp.where(is_last, label_table, hand_over(fates_now))
        terms = forward(kernel, carried * scale_v[None, :])
        sums = lax.psum_scatter(terms, "col", scatter_dimension=1, tiled=True)
        return jnp.where(own_valid[None, :], sums / safe_rows[None, :], 0.0)

    fates = lax.fori_loop(0, n_pair, advance, empty)
    mass = jnp.where(own_valid, source_total * own_scale * own_rows, 0.0)
    return (fates[None], mass[None])


LANES = 128
PIECES = 32
HALF = 16
BIG = 1e30
LOG2E = 1.4426950408889634
MESH = pl.DeviceIdType.MESH


def split3(a):
    first = a.astype(jnp.bfloat16)
    rest = a - first.astype(jnp.float32)
    second = rest.astype(jnp.bfloat16)
    third = (rest - second.astype(jnp.float32)).astype(jnp.bfloat16)
    return first, second, third


def split2(a):
    first = a.astype(jnp.bfloat16)
    return first, (a - first.astype(jnp.float32)).astype(jnp.bfloat16)


def dot(a, b, dims):
    return lax.dot_general(a, b, (dims, ((), ())), preferred_element_type=jnp.float32)


def packed(block, extra):
    low = block[:HALF]
    rest = block.shape[0] - HALF
    fill = jnp.zeros((HALF - rest - 1, block.shape[1]), jnp.float32)
    high = jnp.concatenate([block[HALF:], extra, fill], axis=0)
    return jnp.concatenate([low, high], axis=1)


def unpacked(ref, time, n_block):
    lows, highs = [], []
    lane = lax.broadcasted_iota(jnp.int32, (HALF, LANES), 1)
    for slot in range(0, n_block, 2):
        a, b = ref[time * n_block + slot], ref[time * n_block + slot + 1]
        swap_a, swap_b = pltpu.roll(a, LANES // 2, 1), pltpu.roll(b, LANES // 2, 1)
        lows.append(jnp.where(lane < LANES // 2, a, swap_b))
        highs.append(jnp.where(lane < LANES // 2, swap_a, b))
    low, high = jnp.concatenate(lows, axis=1), jnp.concatenate(highs, axis=1)
    return jnp.concatenate([low, high], axis=0)


def fused(
    sizes,
    counts_in,
    coords_in,
    final_in,
    growth_in,
    labels_in,
    fates_ref,
    mass_ref,
    counts_ref,
    coords_ref,
    final_ref,
    growth_ref,
    labels_ref,
    xg,
    k1,
    k2,
    fin,
    fout,
    own_sems,
    x_send,
    r_send,
    r_recv,
    x_recv,
    f_send,
    f_recv,
    ready,
):
    n_pair, n_row, n_col, tile = sizes
    n_block = n_row * n_col
    cells = n_block * tile
    pca = coords_in.shape[0]
    pair_at = lax.axis_index("pair")
    row_at = lax.axis_index("row")
    col_at = lax.axis_index("col")

    def place(slot):
        along, down = divmod(slot, n_row)
        return (row_at + down) % n_row, (col_at + along) % n_col

    barrier = pltpu.get_barrier_semaphore()
    mine = col_at * n_row + row_at

    def fed(pair):
        return [other for other in range(pair + 1) if other == pair or other % 2]

    def feeding(pair):
        return [other for other in range(n_pair) if pair in fed(other)]

    def met(pair):
        return [other for other in range(n_pair) if other in fed(pair) + feeding(pair)]

    def at(block):
        return block % n_row, block // n_row

    def signal(semaphore, pair, block):
        pl.semaphore_signal(
            semaphore, inc=1, device_id=(pair, *at(block)), device_id_type=MESH
        )

    def loop(start, stop, act):
        def step(block, carry):
            act(block)
            return carry

        lax.fori_loop(start, stop, step, 0)

    count_load = pltpu.make_async_copy(counts_in, counts_ref, own_sems.at[4])
    own_loads = (
        pltpu.make_async_copy(coords_in, coords_ref, own_sems.at[0]),
        pltpu.make_async_copy(growth_in, growth_ref, own_sems.at[1]),
        pltpu.make_async_copy(final_in, final_ref, own_sems.at[2]),
        pltpu.make_async_copy(labels_in, labels_ref, own_sems.at[3]),
    )
    for load in own_loads:
        load.start()
    count_load.start()

    def block_copy(time, pair, block):
        row, col = at(block)
        there = (col_at - col) % n_col * n_row + (row_at - row) % n_row
        return pltpu.make_async_remote_copy(
            src_ref=xg.at[time * n_block],
            dst_ref=xg.at[time * n_block + there],
            send_sem=x_send,
            recv_sem=x_recv.at[time],
            device_id=(pair, row, col),
            device_id_type=MESH,
        )

    below = jnp.maximum(pair_at - 1, 0)

    def blocks(time, start, number):
        return xg.at[pl.ds(time * n_block + start, number)]

    def relay(time):
        return pltpu.make_async_remote_copy(
            src_ref=blocks(time, 0, 2 * n_block),
            dst_ref=blocks(time, 0, 2 * n_block),
            send_sem=r_send,
            recv_sem=r_recv,
            device_id=(below, row_at, col_at),
            device_id_type=MESH,
        )

    f_copy = pltpu.make_async_remote_copy(
        src_ref=fout,
        dst_ref=fin,
        send_sem=f_send,
        recv_sem=f_recv,
        device_id=(below, row_at, col_at),
        device_id_type=MESH,
    )

    def arrival(buffer, sem):
        return pltpu.make_async_remote_copy(
            src_ref=buffer,
            dst_ref=buffer,
            send_sem=x_send,
            recv_sem=sem,
            device_id=(pair_at, row_at, col_at),
            device_id_type=MESH,
        )

    def bound(own, pair):
        shift = n_row * (own // 2 - pair // 2) + (pair < own)
        return jnp.minimum(jnp.maximum(mine + shift, 0), n_block)

    def send(own, is_upper):
        for pair in fed(own):

            def step(block, pair=pair):
                block_copy(own, pair, block).start()
                if pair == own and own % 2:
                    block_copy(n_pair, pair, block).start()

            if is_upper:
                loop(mine + 1 if pair == own else bound(own, pair), n_block, step)
            else:
                loop(0, mine if pair == own else bound(own, pair), step)

    def body(first):
        for pair in met(first):
            start = mine + 1 if pair == first else bound(first, pair)
            loop(start, n_block, functools.partial(signal, barrier, pair))
        if first % 2 == 0:
            signal(barrier, first + 1, mine)
        under = sum(mine if pair == first else bound(first, pair) for pair in met(first))
        if first % 2:
            pl.semaphore_wait(barrier, under + 1)
        else:
            pl.when(under > 0)(lambda: pl.semaphore_wait(barrier, under))
        for pair in feeding(first):
            stop = mine if pair == first else bound(first, pair)
            loop(0, stop, functools.partial(signal, ready, pair))
        for load in own_loads:
            load.wait()
        xg[first * n_block] = packed(coords_ref[:, 0, :], growth_ref[...])
        if first % 2:
            xg[n_pair * n_block] = packed(final_ref[...], labels_ref[...].astype(jnp.float32))
        send(first, False)
        over = sum(
            n_block - (mine + 1 if pair == first else bound(first, pair)) for pair in fed(first)
        )
        pl.when(over > 0)(lambda: pl.semaphore_wait(ready, over))
        send(first, True)
        count_load.wait()
        odd = first % 2 == 1
        stop = n_pair if odd else first + 2
        for time in range(first, n_pair + 1 if odd else first + 1):
            start = 1 if time in (first, n_pair) else 0
            arrival(blocks(time, start, n_block - start), x_recv.at[time]).wait_recv()
        if odd:
            relay(first).start()
        else:
            arrival(blocks(first + 1, 0, 2 * n_block), r_recv).wait_recv()

        lane = lax.broadcasted_iota(jnp.int32, (1, LANES), 1)
        pieces = []
        for slot in range(0, n_block, 2):
            bases = []
            for part in (slot, slot + 1):
                row, col = place(part)
                bases.append((row * n_col + col) * tile)
            pieces.append(jnp.where(lane < tile, bases[0] + lane, bases[1] + lane - tile))
        index = jnp.concatenate(pieces, axis=1)
        feature = lax.broadcasted_iota(jnp.int32, (PIECES, cells), 0)

        def joined(parts):
            return jnp.concatenate(list(parts), axis=1)

        lefts, rights, valid, extra = {}, {}, {}, {}
        for time in range(first, stop + 1):
            valid[time] = index < counts_ref[time]
            z = unpacked(xg, time, n_block)
            extra[time] = z[pca : pca + 1]
            z = jnp.where(feature < pca, z, 0.0)
            norm = jnp.sum(z * z, axis=0, keepdims=True) * LOG2E
            if time < stop:
                a = jnp.where(
                    feature < pca, z * (2.0 * LOG2E), jnp.where(feature == pca, -norm, 1.0)
                )
                a1, a2, a3 = split3(a)
                rights[time] = jnp.concatenate([a1, a2, a1, a2, a3, a1], axis=0)
            if time > first:
                low = jnp.where(valid[time], -norm, -BIG)
                b = jnp.where(feature < pca, z, jnp.where(feature == pca, 1.0, low))
                b1, b2, b3 = split3(b)
                lefts[time] = jnp.concatenate([b1, b1, b2, b2, b1, b3], axis=0)

        def numbers(time):
            return counts_ref[time].astype(jnp.float32)

        def plan(pair):
            total = jnp.zeros((8, cells), jnp.float32)
            for j in range(cells // LANES):
                rows = slice(j * LANES, (j + 1) * LANES)
                values = jnp.exp2(dot(lefts[pair + 1][:, rows], rights[pair], ((0,), (0,))))
                for k in range(LANES // 8):
                    total = total + values[k * 8 : (k + 1) * 8]
                high, low = split2(values)
                k1[pair, rows, :] = high
                k2[pair, rows, :] = low
            total = jnp.sum(total, axis=0, keepdims=True)
            share = jnp.sqrt(extra[pair] / numbers(pair))
            scale_u = jnp.where(valid[pair], share * lax.rsqrt(total), 0.0)
            u1, u2 = split2(jnp.broadcast_to(scale_u, (CLASSES, cells)))
            column = dot(jnp.concatenate([u1, u2], axis=0), k1[pair], ((1,), (1,)))
            column_low = dot(u1, k2[pair], ((1,), (1,)))
            column = column[:1] + column[CLASSES : CLASSES + 1] + column_low[:1]
            column = jnp.where(valid[pair + 1], column, 1.0)
            power = jnp.log2(column) + jnp.log2(jnp.full((1, cells), numbers(pair + 1)))
            scale_v = jnp.where(valid[pair + 1], jnp.exp2(-target_power * power), 0.0)
            row_totals = transported(pair, jnp.broadcast_to(scale_v, (CLASSES, cells)), cells)[:1]
            return scale_u, scale_v, row_totals

        def transported(pair, weights, width):
            w1, w2 = split2(weights)
            both = dot(jnp.concatenate([w1, w2], axis=0), k1[pair, :, :width], ((1,), (0,)))
            half = weights.shape[0]
            return both[:half] + both[half:] + dot(w1, k2[pair, :, :width], ((1,), (0,)))

        def advance(pair, scale_v, row_totals, fates):
            width = LANES if pair == first else cells
            share = jnp.where(valid[pair], 1.0 / row_totals, 0.0)
            return transported(pair, fates * scale_v, width) * share[:, :width]

        plans = {}
        if stop == n_pair:
            classes = lax.broadcasted_iota(jnp.int32, (CLASSES, cells), 0).astype(jnp.float32)
            fates = jnp.where((extra[n_pair] == classes) & valid[n_pair], 1.0, 0.0)
        for pair in range(stop - 1, first, -1):
            plans[pair] = plan(pair)
        if stop < n_pair:
            plans[first] = plan(first)
            f_copy.wait_recv()
            fates = fin[...]
        for pair in range(stop - 1, first, -1):
            fates = advance(pair, plans[pair][1], plans[pair][2], fates)
        if odd and first + 1 < n_pair:
            fout[...] = fates
            f_copy.start()
        if stop == n_pair:
            plans[first] = plan(first)
        scale_u, scale_v, row_totals = plans[first]
        fates = advance(first, scale_v, row_totals, fates)
        mass = jnp.where(valid[first], numbers(first) * scale_u * row_totals, 0.0)
        fates_ref[0] = fates[:, :tile]
        mass_ref[...] = mass[:, :tile]
        if odd:
            relay(first).wait_send()
            if first + 1 < n_pair:
                f_copy.wait_send()
        number = len(fed(first)) * n_block - 1 + (n_block - 1) * odd
        arrival(blocks(0, 0, number), x_recv.at[0]).wait_send()

    for pair in range(n_pair):

        @pl.when(pair_at == pair)
        def _(pair=pair):
            body(pair)


def per_device_fused(coords, final_coords, growth, counts, labels):
    pca, tile = coords.shape[1], coords.shape[2]
    n_pair = lax.axis_size("pair")
    n_row = lax.axis_size("row")
    n_col = lax.axis_size("col")
    n_block = n_row * n_col
    cells = n_block * tile
    vmem = pl.BlockSpec(memory_space=pltpu.VMEM)
    dma = pltpu.SemaphoreType.DMA
    return pl.pallas_call(
        functools.partial(fused, (n_pair, n_row, n_col, tile)),
        out_shape=(
            pltpu.VMEM((1, CLASSES, tile), jnp.float32),
            pltpu.VMEM((1, tile), jnp.float32),
        ),
        in_specs=[pl.BlockSpec(memory_space=pl.ANY)] * 5,
        out_specs=(vmem, vmem),
        scratch_shapes=[
            pltpu.SMEM((n_pair + 1,), jnp.int32),
            pltpu.VMEM((pca, 1, tile), jnp.float32),
            pltpu.VMEM((pca, tile), jnp.float32),
            pltpu.VMEM((1, tile), jnp.float32),
            pltpu.VMEM((1, tile), jnp.int32),
            pltpu.VMEM(((n_pair + 1) * n_block, HALF, LANES), jnp.float32),
            pltpu.VMEM((n_pair, cells, cells), jnp.bfloat16),
            pltpu.VMEM((n_pair, cells, cells), jnp.bfloat16),
            pltpu.VMEM((CLASSES, cells), jnp.float32),
            pltpu.VMEM((CLASSES, cells), jnp.float32),
            dma((5,)),
            dma,
            dma,
            dma,
            dma((n_pair + 1,)),
            dma,
            dma,
            pltpu.SemaphoreType.REGULAR,
        ],
        compiler_params=pltpu.CompilerParams(collective_id=0, has_side_effects=True),
    )(counts, jnp.transpose(coords, (1, 0, 2)), final_coords, growth, labels[None, :])


def solution(mesh):
    placed = (
        P("pair", None, ("row", "col")),
        P(None, ("row", "col")),
        P("pair", ("row", "col")),
        P(),
        P(("row", "col")),
    )
    out = (P("pair", None, ("row", "col")), P("pair", ("row", "col")))

    def whole(coords, final_coords, growth, counts, labels):
        cells = coords.shape[2]
        pairs = mesh.shape["pair"]
        blocks = mesh.shape["row"] * mesh.shape["col"]
        fits = (
            2 * cells == LANES * blocks
            and blocks % 2 == 0
            and pairs % 2 == 0
            and coords.shape[0] == pairs
            and coords.shape[1] + 2 <= PIECES
            and 4 * pairs * cells * cells <= FUSED_BYTES
        )
        body = per_device_fused if fits else per_device
        return jax.shard_map(
            body, mesh=mesh, in_specs=placed, out_specs=out, check_vma=False
        )(coords, final_coords, growth, counts, labels)

    return whole
```

```python
import functools
import jax
import jax.numpy as jnp
from jax import lax
from jax.experimental import pallas as pl
from jax.experimental.pallas import tpu as pltpu
from jax.sharding import PartitionSpec as P

CLASSES = 16
FUSED_BYTES = 16 * 1024 * 1024


cost_scale = 1.0
source_power = 0.5
target_power = 50.0 / 51.0


def shifted_2(block, axis, distance):
    devices = range(lax.axis_size(axis))
    route = [(i - distance, i) for i in devices if i - distance in devices]
    return lax.ppermute(block, axis, route)


def kernel_tile(sources, targets):
    cross = lax.dot_general(
        sources,
        targets,
        (((0,), (0,)), ((), ())),
        precision=lax.Precision.HIGHEST,
        preferred_element_type=jnp.float32,
    )
    source_norms = jnp.sum(sources * sources, axis=0)
    target_norms = jnp.sum(targets * targets, axis=0)
    return jnp.exp(-(source_norms[:, None] + target_norms[None, :] - 2.0 * cross) / cost_scale)


def forward(kernel, weights):
    return lax.dot_general(
        weights,
        kernel,
        (((1,), (1,)), ((), ())),
        precision=lax.Precision.HIGHEST,
        preferred_element_type=jnp.float32,
    )


def backward(kernel, scales):
    return jnp.dot(
        scales, kernel, precision=lax.Precision.HIGHEST, preferred_element_type=jnp.float32
    )


def per_device(coords, final_coords, growth, counts, labels):
    tile = coords.shape[2]
    n_pair = lax.axis_size("pair")
    n_row = lax.axis_size("row")
    n_col = lax.axis_size("col")
    pair_at = lax.axis_index("pair")
    row_at = lax.axis_index("row")
    col_at = lax.axis_index("col")
    source_count = n_col * tile
    target_count = n_row * tile
    own_coords = coords[0]
    sources, source_growth = (
        lax.all_gather(own_coords, "col", axis=1, tiled=True),
        lax.all_gather(growth[0], "col", axis=0, tiled=True),
    )
    shifted = shifted_2(own_coords, "pair", -1)
    is_last = pair_at == n_pair - 1
    own_targets = jnp.where(is_last, final_coords, shifted)
    label_values = labels.astype(jnp.float32)
    position = lax.iota(jnp.int32, target_count)
    targets, target_labels = (
        lax.all_gather(own_targets, "row", axis=1, tiled=True),
        lax.all_gather(label_values, "row", axis=0, tiled=True),
    )
    target_index = position // tile * (n_col * tile) + col_at * tile + position % tile

    def hand_over(fates_now):
        incoming = shifted_2(fates_now, "pair", -1)
        return lax.all_gather(incoming, "row", axis=1, tiled=True)

    source_number = counts[pair_at]
    target_number = counts[pair_at + 1]
    source_total = source_number.astype(jnp.float32)
    target_total = target_number.astype(jnp.float32)
    source_index = row_at * source_count + lax.iota(jnp.int32, source_count)
    source_valid = source_index < source_number
    target_valid = target_index < target_number
    kernel = kernel_tile(sources, targets)
    start_terms = forward(kernel, target_valid.astype(jnp.float32)[None, :])[0]
    start_rows = lax.psum(start_terms, "col")
    source_mass = jnp.where(source_valid, source_growth / source_total, 0.0)
    scale_u = jnp.where(source_valid, jnp.power(source_mass / start_rows, source_power), 0.0)
    column_terms = backward(kernel, scale_u)
    column_totals = lax.psum(column_terms, "row")
    target_mass = target_valid.astype(jnp.float32) / target_total
    scale_v = jnp.where(target_valid, jnp.power(target_mass / column_totals, target_power), 0.0)
    own_offset = col_at * tile
    own_valid = lax.dynamic_slice_in_dim(source_valid, own_offset, tile, 0)
    own_scale = lax.dynamic_slice_in_dim(scale_u, own_offset, tile, 0)
    class_values = lax.iota(jnp.int32, CLASSES).astype(jnp.float32)
    label_table = jnp.where(
        (target_labels[None, :] == class_values[:, None]) & target_valid[None, :], 1.0, 0.0
    ).astype(jnp.float32)
    empty = jnp.zeros((CLASSES, tile), jnp.float32)
    final_terms = forward(kernel, scale_v[None, :])[0]
    final_rows = lax.psum(final_terms, "col")
    own_rows = lax.dynamic_slice_in_dim(final_rows, own_offset, tile, 0)
    safe_rows = jnp.where(own_valid, own_rows, 1.0)

    def advance(turn, fates_now):
        carried = jnp.where(is_last, label_table, hand_over(fates_now))
        terms = forward(kernel, carried * scale_v[None, :])
        sums = lax.psum_scatter(terms, "col", scatter_dimension=1, tiled=True)
        return jnp.where(own_valid[None, :], sums / safe_rows[None, :], 0.0)

    fates = lax.fori_loop(0, n_pair, advance, empty)
    mass = jnp.where(own_valid, source_total * own_scale * own_rows, 0.0)
    return (fates[None], mass[None])


LANES = 128
PIECES = 32
HALF = 16
BIG = 1e30
LOG2E = 1.4426950408889634
MESH = pl.DeviceIdType.MESH


def split3(a):
    first = a.astype(jnp.bfloat16)
    rest = a - first.astype(jnp.float32)
    second = rest.astype(jnp.bfloat16)
    third = (rest - second.astype(jnp.float32)).astype(jnp.bfloat16)
    return first, second, third


def split2(a):
    first = a.astype(jnp.bfloat16)
    return first, (a - first.astype(jnp.float32)).astype(jnp.bfloat16)


def dot(a, b, dims):
    return lax.dot_general(a, b, (dims, ((), ())), preferred_element_type=jnp.float32)


def packed(block, extra):
    low = block[:HALF]
    rest = block.shape[0] - HALF
    fill = jnp.zeros((HALF - rest - 1, block.shape[1]), jnp.float32)
    high = jnp.concatenate([block[HALF:], extra, fill], axis=0)
    return jnp.concatenate([low, high], axis=1)


def unpacked(ref, time, n_block):
    lows, highs = [], []
    lane = lax.broadcasted_iota(jnp.int32, (HALF, LANES), 1)
    for slot in range(0, n_block, 2):
        a, b = ref[time * n_block + slot], ref[time * n_block + slot + 1]
        swap_a, swap_b = pltpu.roll(a, LANES // 2, 1), pltpu.roll(b, LANES // 2, 1)
        lows.append(jnp.where(lane < LANES // 2, a, swap_b))
        highs.append(jnp.where(lane < LANES // 2, swap_a, b))
    low, high = jnp.concatenate(lows, axis=1), jnp.concatenate(highs, axis=1)
    return jnp.concatenate([low, high], axis=0)


def fused(
    sizes,
    counts_in,
    coords_in,
    final_in,
    growth_in,
    labels_in,
    fates_ref,
    mass_ref,
    counts_ref,
    coords_ref,
    final_ref,
    growth_ref,
    labels_ref,
    xg,
    k1,
    k2,
    fin,
    fout,
    own_sems,
    x_send,
    r_send,
    r_recv,
    x_recv,
    f_send,
    f_recv,
    ready,
):
    n_pair, n_row, n_col, tile = sizes
    n_block = n_row * n_col
    cells = n_block * tile
    pca = coords_in.shape[0]
    pair_at = lax.axis_index("pair")
    row_at = lax.axis_index("row")
    col_at = lax.axis_index("col")

    def place(slot):
        along, down = divmod(slot, n_row)
        return (row_at + down) % n_row, (col_at + along) % n_col

    barrier = pltpu.get_barrier_semaphore()
    mine = col_at * n_row + row_at

    def fed(pair):
        return [other for other in range(pair + 1) if other == pair or other % 2]

    def feeding(pair):
        return [other for other in range(n_pair) if pair in fed(other)]

    def met(pair):
        return [other for other in range(n_pair) if other in fed(pair) + feeding(pair)]

    def at(block):
        return block % n_row, block // n_row

    def signal(semaphore, pair, block):
        pl.semaphore_signal(
            semaphore, inc=1, device_id=(pair, *at(block)), device_id_type=MESH
        )

    def loop(start, stop, act):
        def step(block, carry):
            act(block)
            return carry

        lax.fori_loop(start, stop, step, 0)

    count_load = pltpu.make_async_copy(counts_in, counts_ref, own_sems.at[4])
    own_loads = (
        pltpu.make_async_copy(coords_in, coords_ref, own_sems.at[0]),
        pltpu.make_async_copy(growth_in, growth_ref, own_sems.at[1]),
        pltpu.make_async_copy(final_in, final_ref, own_sems.at[2]),
        pltpu.make_async_copy(labels_in, labels_ref, own_sems.at[3]),
    )
    for load in own_loads:
        load.start()
    count_load.start()

    def block_copy(time, pair, block):
        row, col = at(block)
        there = (col_at - col) % n_col * n_row + (row_at - row) % n_row
        return pltpu.make_async_remote_copy(
            src_ref=xg.at[time * n_block],
            dst_ref=xg.at[time * n_block + there],
            send_sem=x_send,
            recv_sem=x_recv.at[time],
            device_id=(pair, row, col),
            device_id_type=MESH,
        )

    below = jnp.maximum(pair_at - 1, 0)

    def blocks(time, start, number):
        return xg.at[pl.ds(time * n_block + start, number)]

    def relay(time):
        return pltpu.make_async_remote_copy(
            src_ref=blocks(time, 0, 2 * n_block),
            dst_ref=blocks(time, 0, 2 * n_block),
            send_sem=r_send,
            recv_sem=r_recv,
            device_id=(below, row_at, col_at),
            device_id_type=MESH,
        )

    f_copy = pltpu.make_async_remote_copy(
        src_ref=fout,
        dst_ref=fin,
        send_sem=f_send,
        recv_sem=f_recv,
        device_id=(below, row_at, col_at),
        device_id_type=MESH,
    )

    def arrival(buffer, sem):
        return pltpu.make_async_remote_copy(
            src_ref=buffer,
            dst_ref=buffer,
            send_sem=x_send,
            recv_sem=sem,
            device_id=(pair_at, row_at, col_at),
            device_id_type=MESH,
        )

    def bound(own, pair):
        shift = n_row * (own // 2 - pair // 2) + (pair < own)
        return jnp.minimum(jnp.maximum(mine + shift, 0), n_block)

    def send(own, is_upper):
        for pair in fed(own):

            def step(block, pair=pair):
                block_copy(own, pair, block).start()
                if pair == own and own % 2:
                    block_copy(n_pair, pair, block).start()

            if is_upper:
                loop(mine + 1 if pair == own else bound(own, pair), n_block, step)
            else:
                loop(0, mine if pair == own else bound(own, pair), step)

    def body(first):
        for pair in met(first):
            start = mine + 1 if pair == first else bound(first, pair)
            loop(start, n_block, functools.partial(signal, barrier, pair))
        if first % 2 == 0:
            signal(barrier, first + 1, mine)
        under = sum(mine if pair == first else bound(first, pair) for pair in met(first))
        if first % 2:
            pl.semaphore_wait(barrier, under + 1)
        else:
            pl.when(under > 0)(lambda: pl.semaphore_wait(barrier, under))
        for pair in feeding(first):
            stop = mine if pair == first else bound(first, pair)
            loop(0, stop, functools.partial(signal, ready, pair))
        for load in own_loads:
            load.wait()
        xg[first * n_block] = packed(coords_ref[:, 0, :], growth_ref[...])
        if first % 2:
            xg[n_pair * n_block] = packed(final_ref[...], labels_ref[...].astype(jnp.float32))
        send(first, False)
        over = sum(
            n_block - (mine + 1 if pair == first else bound(first, pair)) for pair in fed(first)
        )
        pl.when(over > 0)(lambda: pl.semaphore_wait(ready, over))
        send(first, True)
        count_load.wait()
        odd = first % 2 == 1
        stop = n_pair if odd else first + 2
        for time in range(first, n_pair + 1 if odd else first + 1):
            start = 1 if time in (first, n_pair) else 0
            arrival(blocks(time, start, n_block - start), x_recv.at[time]).wait_recv()
        if odd:
            relay(first).start()
        else:
            arrival(blocks(first + 1, 0, 2 * n_block), r_recv).wait_recv()

        lane = lax.broadcasted_iota(jnp.int32, (1, LANES), 1)
        pieces = []
        for slot in range(0, n_block, 2):
            bases = []
            for part in (slot, slot + 1):
                row, col = place(part)
                bases.append((row * n_col + col) * tile)
            pieces.append(jnp.where(lane < tile, bases[0] + lane, bases[1] + lane - tile))
        index = jnp.concatenate(pieces, axis=1)
        feature = lax.broadcasted_iota(jnp.int32, (PIECES, cells), 0)

        def joined(parts):
            return jnp.concatenate(list(parts), axis=1)

        lefts, rights, valid, extra = {}, {}, {}, {}
        for time in range(first, stop + 1):
            valid[time] = index < counts_ref[time]
            z = unpacked(xg, time, n_block)
            extra[time] = z[pca : pca + 1]
            z = jnp.where(feature < pca, z, 0.0)
            norm = jnp.sum(z * z, axis=0, keepdims=True) * LOG2E
            if time < stop:
                a = jnp.where(
                    feature < pca, z * (2.0 * LOG2E), jnp.where(feature == pca, -norm, 1.0)
                )
                a1, a2, a3 = split3(a)
                rights[time] = jnp.concatenate([a1, a2, a1, a2, a3, a1], axis=0)
            if time > first:
                low = jnp.where(valid[time], -norm, -BIG)
                b = jnp.where(feature < pca, z, jnp.where(feature == pca, 1.0, low))
                b1, b2, b3 = split3(b)
                lefts[time] = jnp.concatenate([b1, b1, b2, b2, b1, b3], axis=0)

        def numbers(time):
            return counts_ref[time].astype(jnp.float32)

        def plan(pair):
            total = jnp.zeros((8, cells), jnp.float32)
            for j in range(cells // LANES):
                rows = slice(j * LANES, (j + 1) * LANES)
                values = jnp.exp2(dot(lefts[pair + 1][:, rows], rights[pair], ((0,), (0,))))
                for k in range(LANES // 8):
                    total = total + values[k * 8 : (k + 1) * 8]
                high, low = split2(values)
                k1[pair, rows, :] = high
                k2[pair, rows, :] = low
            total = jnp.sum(total, axis=0, keepdims=True)
            share = jnp.sqrt(extra[pair] / numbers(pair))
            scale_u = jnp.where(valid[pair], share * lax.rsqrt(total), 0.0)
            u1, u2 = split2(jnp.broadcast_to(scale_u, (CLASSES, cells)))
            column = dot(jnp.concatenate([u1, u2], axis=0), k1[pair], ((1,), (1,)))
            column_low = dot(u1, k2[pair], ((1,), (1,)))
            column = column[:1] + column[CLASSES : CLASSES + 1] + column_low[:1]
            column = jnp.where(valid[pair + 1], column, 1.0)
            power = jnp.log2(column) + jnp.log2(jnp.full((1, cells), numbers(pair + 1)))
            scale_v = jnp.where(valid[pair + 1], jnp.exp2(-target_power * power), 0.0)
            row_totals = transported(pair, jnp.broadcast_to(scale_v, (CLASSES, cells)), cells)[:1]
            return scale_u, scale_v, row_totals

        def transported(pair, weights, width):
            w1, w2 = split2(weights)
            both = dot(jnp.concatenate([w1, w2], axis=0), k1[pair, :, :width], ((1,), (0,)))
            half = weights.shape[0]
            return both[:half] + both[half:] + dot(w1, k2[pair, :, :width], ((1,), (0,)))

        def advance(pair, scale_v, row_totals, fates):
            width = LANES if pair == first else cells
            share = jnp.where(valid[pair], 1.0 / row_totals, 0.0)
            return transported(pair, fates * scale_v, width) * share[:, :width]

        plans = {}
        if stop == n_pair:
            classes = lax.broadcasted_iota(jnp.int32, (CLASSES, cells), 0).astype(jnp.float32)
            fates = jnp.where((extra[n_pair] == classes) & valid[n_pair], 1.0, 0.0)
        for pair in range(stop - 1, first, -1):
            plans[pair] = plan(pair)
        if stop < n_pair:
            plans[first] = plan(first)
            f_copy.wait_recv()
            fates = fin[...]
        for pair in range(stop - 1, first, -1):
            fates = advance(pair, plans[pair][1], plans[pair][2], fates)
        if odd and first + 1 < n_pair:
            fout[...] = fates
            f_copy.start()
        if stop == n_pair:
            plans[first] = plan(first)
        scale_u, scale_v, row_totals = plans[first]
        fates = advance(first, scale_v, row_totals, fates)
        mass = jnp.where(valid[first], numbers(first) * scale_u * row_totals, 0.0)
        fates_ref[0] = fates[:, :tile]
        mass_ref[...] = mass[:, :tile]
        if odd:
            relay(first).wait_send()
            if first + 1 < n_pair:
                f_copy.wait_send()
        number = len(fed(first)) * n_block - 1 + (n_block - 1) * odd
        arrival(blocks(0, 0, number), x_recv.at[0]).wait_send()

    for pair in range(n_pair):

        @pl.when(pair_at == pair)
        def _(pair=pair):
            body(pair)


def written(fates_ref, mass_ref, fates_out, mass_out, sems):
    copies = (
        pltpu.make_async_copy(mass_ref, mass_out, sems.at[0]),
        pltpu.make_async_copy(fates_ref, fates_out, sems.at[1]),
    )
    for copy in copies:
        copy.start()
    for copy in copies:
        copy.wait()


def per_device_fused(coords, final_coords, growth, counts, labels):
    pca, tile = coords.shape[1], coords.shape[2]
    n_pair = lax.axis_size("pair")
    n_row = lax.axis_size("row")
    n_col = lax.axis_size("col")
    n_block = n_row * n_col
    cells = n_block * tile
    vmem = pl.BlockSpec(memory_space=pltpu.VMEM)
    dma = pltpu.SemaphoreType.DMA
    fates, mass = pl.pallas_call(
        functools.partial(fused, (n_pair, n_row, n_col, tile)),
        out_shape=(
            pltpu.VMEM((1, CLASSES, tile), jnp.float32),
            pltpu.VMEM((1, tile), jnp.float32),
        ),
        in_specs=[pl.BlockSpec(memory_space=pl.ANY)] * 5,
        out_specs=(vmem, vmem),
        scratch_shapes=[
            pltpu.SMEM((n_pair + 1,), jnp.int32),
            pltpu.VMEM((pca, 1, tile), jnp.float32),
            pltpu.VMEM((pca, tile), jnp.float32),
            pltpu.VMEM((1, tile), jnp.float32),
            pltpu.VMEM((1, tile), jnp.int32),
            pltpu.VMEM(((n_pair + 1) * n_block, HALF, LANES), jnp.float32),
            pltpu.VMEM((n_pair, cells, cells), jnp.bfloat16),
            pltpu.VMEM((n_pair, cells, cells), jnp.bfloat16),
            pltpu.VMEM((CLASSES, cells), jnp.float32),
            pltpu.VMEM((CLASSES, cells), jnp.float32),
            dma((5,)),
            dma,
            dma,
            dma,
            dma((n_pair + 1,)),
            dma,
            dma,
            pltpu.SemaphoreType.REGULAR,
        ],
        compiler_params=pltpu.CompilerParams(collective_id=0, has_side_effects=True),
    )(counts, jnp.transpose(coords, (1, 0, 2)), final_coords, growth, labels[None, :])
    return pl.pallas_call(
        written,
        out_shape=(
            jax.ShapeDtypeStruct(fates.shape, jnp.float32),
            jax.ShapeDtypeStruct(mass.shape, jnp.float32),
        ),
        in_specs=(vmem, vmem),
        out_specs=(pl.BlockSpec(memory_space=pl.ANY), pl.BlockSpec(memory_space=pl.ANY)),
        scratch_shapes=[dma((2,))],
    )(*(pltpu.with_memory_space_constraint(x, pltpu.VMEM) for x in (fates, mass)))


def solution(mesh):
    placed = (
        P("pair", None, ("row", "col")),
        P(None, ("row", "col")),
        P("pair", ("row", "col")),
        P(),
        P(("row", "col")),
    )
    out = (P("pair", None, ("row", "col")), P("pair", ("row", "col")))

    def whole(coords, final_coords, growth, counts, labels):
        cells = coords.shape[2]
        pairs = mesh.shape["pair"]
        blocks = mesh.shape["row"] * mesh.shape["col"]
        fits = (
            2 * cells == LANES * blocks
            and blocks % 2 == 0
            and pairs % 2 == 0
            and coords.shape[0] == pairs
            and coords.shape[1] + 2 <= PIECES
            and 4 * pairs * cells * cells <= FUSED_BYTES
        )
        body = per_device_fused if fits else per_device
        return jax.shard_map(
            body, mesh=mesh, in_specs=placed, out_specs=out, check_vma=False
        )(coords, final_coords, growth, counts, labels)

    return whole
```

```python
import functools
import jax
import jax.numpy as jnp
from jax import lax
from jax.experimental import pallas as pl
from jax.experimental.pallas import tpu as pltpu
from jax.sharding import PartitionSpec as P

CLASSES = 16
FUSED_BYTES = 16 * 1024 * 1024


cost_scale = 1.0
source_power = 0.5
target_power = 50.0 / 51.0


def shifted_2(block, axis, distance):
    devices = range(lax.axis_size(axis))
    route = [(i - distance, i) for i in devices if i - distance in devices]
    return lax.ppermute(block, axis, route)


def kernel_tile(sources, targets):
    cross = lax.dot_general(
        sources,
        targets,
        (((0,), (0,)), ((), ())),
        precision=lax.Precision.HIGHEST,
        preferred_element_type=jnp.float32,
    )
    source_norms = jnp.sum(sources * sources, axis=0)
    target_norms = jnp.sum(targets * targets, axis=0)
    return jnp.exp(-(source_norms[:, None] + target_norms[None, :] - 2.0 * cross) / cost_scale)


def forward(kernel, weights):
    return lax.dot_general(
        weights,
        kernel,
        (((1,), (1,)), ((), ())),
        precision=lax.Precision.HIGHEST,
        preferred_element_type=jnp.float32,
    )


def backward(kernel, scales):
    return jnp.dot(
        scales, kernel, precision=lax.Precision.HIGHEST, preferred_element_type=jnp.float32
    )


def per_device(coords, final_coords, growth, counts, labels):
    tile = coords.shape[2]
    n_pair = lax.axis_size("pair")
    n_row = lax.axis_size("row")
    n_col = lax.axis_size("col")
    pair_at = lax.axis_index("pair")
    row_at = lax.axis_index("row")
    col_at = lax.axis_index("col")
    source_count = n_col * tile
    target_count = n_row * tile
    own_coords = coords[0]
    sources, source_growth = (
        lax.all_gather(own_coords, "col", axis=1, tiled=True),
        lax.all_gather(growth[0], "col", axis=0, tiled=True),
    )
    shifted = shifted_2(own_coords, "pair", -1)
    is_last = pair_at == n_pair - 1
    own_targets = jnp.where(is_last, final_coords, shifted)
    label_values = labels.astype(jnp.float32)
    position = lax.iota(jnp.int32, target_count)
    targets, target_labels = (
        lax.all_gather(own_targets, "row", axis=1, tiled=True),
        lax.all_gather(label_values, "row", axis=0, tiled=True),
    )
    target_index = position // tile * (n_col * tile) + col_at * tile + position % tile

    def hand_over(fates_now):
        incoming = shifted_2(fates_now, "pair", -1)
        return lax.all_gather(incoming, "row", axis=1, tiled=True)

    source_number = counts[pair_at]
    target_number = counts[pair_at + 1]
    source_total = source_number.astype(jnp.float32)
    target_total = target_number.astype(jnp.float32)
    source_index = row_at * source_count + lax.iota(jnp.int32, source_count)
    source_valid = source_index < source_number
    target_valid = target_index < target_number
    kernel = kernel_tile(sources, targets)
    start_terms = forward(kernel, target_valid.astype(jnp.float32)[None, :])[0]
    start_rows = lax.psum(start_terms, "col")
    source_mass = jnp.where(source_valid, source_growth / source_total, 0.0)
    scale_u = jnp.where(source_valid, jnp.power(source_mass / start_rows, source_power), 0.0)
    column_terms = backward(kernel, scale_u)
    column_totals = lax.psum(column_terms, "row")
    target_mass = target_valid.astype(jnp.float32) / target_total
    scale_v = jnp.where(target_valid, jnp.power(target_mass / column_totals, target_power), 0.0)
    own_offset = col_at * tile
    own_valid = lax.dynamic_slice_in_dim(source_valid, own_offset, tile, 0)
    own_scale = lax.dynamic_slice_in_dim(scale_u, own_offset, tile, 0)
    class_values = lax.iota(jnp.int32, CLASSES).astype(jnp.float32)
    label_table = jnp.where(
        (target_labels[None, :] == class_values[:, None]) & target_valid[None, :], 1.0, 0.0
    ).astype(jnp.float32)
    empty = jnp.zeros((CLASSES, tile), jnp.float32)
    final_terms = forward(kernel, scale_v[None, :])[0]
    final_rows = lax.psum(final_terms, "col")
    own_rows = lax.dynamic_slice_in_dim(final_rows, own_offset, tile, 0)
    safe_rows = jnp.where(own_valid, own_rows, 1.0)

    def advance(turn, fates_now):
        carried = jnp.where(is_last, label_table, hand_over(fates_now))
        terms = forward(kernel, carried * scale_v[None, :])
        sums = lax.psum_scatter(terms, "col", scatter_dimension=1, tiled=True)
        return jnp.where(own_valid[None, :], sums / safe_rows[None, :], 0.0)

    fates = lax.fori_loop(0, n_pair, advance, empty)
    mass = jnp.where(own_valid, source_total * own_scale * own_rows, 0.0)
    return (fates[None], mass[None])


LANES = 128
PIECES = 32
HALF = 16
BIG = 1e30
LOG2E = 1.4426950408889634
MESH = pl.DeviceIdType.MESH


def split3(a):
    first = a.astype(jnp.bfloat16)
    rest = a - first.astype(jnp.float32)
    second = rest.astype(jnp.bfloat16)
    third = (rest - second.astype(jnp.float32)).astype(jnp.bfloat16)
    return first, second, third


def split2(a):
    first = a.astype(jnp.bfloat16)
    return first, (a - first.astype(jnp.float32)).astype(jnp.bfloat16)


def dot(a, b, dims):
    return lax.dot_general(a, b, (dims, ((), ())), preferred_element_type=jnp.float32)


def packed(block, extra):
    low = block[:HALF]
    rest = block.shape[0] - HALF
    fill = jnp.zeros((HALF - rest - 1, block.shape[1]), jnp.float32)
    high = jnp.concatenate([block[HALF:], extra, fill], axis=0)
    return jnp.concatenate([low, high], axis=1)


def unpacked(ref, start, stop):
    lows, highs = [], []
    lane = lax.broadcasted_iota(jnp.int32, (HALF, LANES), 1)
    for slot in range(start, stop, 2):
        a, b = ref[slot], ref[slot + 1]
        swap_a, swap_b = pltpu.roll(a, LANES // 2, 1), pltpu.roll(b, LANES // 2, 1)
        lows.append(jnp.where(lane < LANES // 2, a, swap_b))
        highs.append(jnp.where(lane < LANES // 2, swap_a, b))
    low, high = jnp.concatenate(lows, axis=1), jnp.concatenate(highs, axis=1)
    return jnp.concatenate([low, high], axis=0)


def fused(
    sizes,
    counts_in,
    coords_in,
    final_in,
    growth_in,
    labels_in,
    fates_ref,
    mass_ref,
    counts_ref,
    coords_ref,
    final_ref,
    growth_ref,
    labels_ref,
    xg,
    kernel,
    k1,
    k2,
    fin,
    fout,
    own_sems,
    x_send,
    r_send,
    x_recv,
    f_send,
    f_recv,
    ready,
):
    n_pair, n_row, n_col, tile = sizes
    n_block = n_row * n_col
    near = n_block - n_row
    cells = n_block * tile
    pca = coords_in.shape[0]
    pair_at = lax.axis_index("pair")
    row_at = lax.axis_index("row")
    col_at = lax.axis_index("col")

    def place(slot):
        along, down = divmod(slot, n_row)
        return (row_at + down) % n_row, (col_at + along) % n_col

    barrier = pltpu.get_barrier_semaphore()
    mine = col_at * n_row + row_at

    def fed(pair):
        return [other for other in range(pair + 1) if other == pair or other % 2]

    def feeding(pair):
        return [other for other in range(n_pair) if pair in fed(other)]

    def met(pair):
        return [other for other in range(n_pair) if other in fed(pair) + feeding(pair)]

    def at(block):
        return block % n_row, block // n_row

    def signal(semaphore, pair, block):
        pl.semaphore_signal(
            semaphore, inc=1, device_id=(pair, *at(block)), device_id_type=MESH
        )

    def loop(start, stop, act):
        def step(block, carry):
            act(block)
            return carry

        lax.fori_loop(start, stop, step, 0)

    count_load = pltpu.make_async_copy(counts_in, counts_ref, own_sems.at[4])
    own_loads = (
        pltpu.make_async_copy(coords_in, coords_ref, own_sems.at[0]),
        pltpu.make_async_copy(growth_in, growth_ref, own_sems.at[1]),
        pltpu.make_async_copy(final_in, final_ref, own_sems.at[2]),
        pltpu.make_async_copy(labels_in, labels_ref, own_sems.at[3]),
    )
    for load in own_loads:
        load.start()
    count_load.start()

    def block_copy(time, pair, block):
        row, col = at(block)
        there = (col_at - col) % n_col * n_row + (row_at - row) % n_row
        return pltpu.make_async_remote_copy(
            src_ref=xg.at[time * n_block],
            dst_ref=xg.at[time * n_block + there],
            send_sem=x_send,
            recv_sem=x_recv.at[time, there // near],
            device_id=(pair, row, col),
            device_id_type=MESH,
        )

    parts = ((0, near), (near, n_block))
    below = jnp.maximum(pair_at - 1, 0)

    def blocks(time, start, number):
        return xg.at[pl.ds(time * n_block + start, number)]

    def relay(time, part):
        start, stop = parts[part]
        block = blocks(time, start, stop - start)
        return pltpu.make_async_remote_copy(
            src_ref=block,
            dst_ref=block,
            send_sem=r_send,
            recv_sem=x_recv.at[time, part],
            device_id=(below, row_at, col_at),
            device_id_type=MESH,
        )

    f_copy = pltpu.make_async_remote_copy(
        src_ref=fout,
        dst_ref=fin,
        send_sem=f_send,
        recv_sem=f_recv,
        device_id=(below, row_at, col_at),
        device_id_type=MESH,
    )

    def arrival(buffer, sem, send_sem=x_send):
        return pltpu.make_async_remote_copy(
            src_ref=buffer,
            dst_ref=buffer,
            send_sem=send_sem,
            recv_sem=sem,
            device_id=(pair_at, row_at, col_at),
            device_id_type=MESH,
        )

    def bound(own, pair):
        shift = 4 * n_row * (own // 2 - pair // 2) + (pair < own)
        return jnp.minimum(jnp.maximum(mine + shift, 0), n_block)

    def send(own, is_upper):
        for pair in fed(own):

            def step(block, pair=pair):
                block_copy(own, pair, block).start()
                if pair == own and own % 2:
                    block_copy(n_pair, pair, block).start()

            under = mine if pair == own else bound(own, pair)
            early = jnp.minimum(under, 1)
            if is_upper:
                loop(early, under, step)
                loop(mine + 1 if pair == own else under, n_block, step)
            else:
                loop(0, early, step)

    def body(first):
        for pair in met(first):
            start = mine + 1 if pair == first else bound(first, pair)
            loop(start, n_block, functools.partial(signal, barrier, pair))
        if first % 2 == 0:
            signal(barrier, first + 1, mine)
        under = sum(mine if pair == first else bound(first, pair) for pair in met(first))
        if first % 2:
            pl.semaphore_wait(barrier, under + 1)
        else:
            pl.when(under > 0)(lambda: pl.semaphore_wait(barrier, under))
        for pair in feeding(first):
            stop = mine if pair == first else bound(first, pair)
            loop(0, stop, functools.partial(signal, ready, pair))
        for load in own_loads:
            load.wait()
        xg[first * n_block] = packed(coords_ref[:, 0, :], growth_ref[...])
        if first % 2:
            xg[n_pair * n_block] = packed(final_ref[...], labels_ref[...].astype(jnp.float32))
        send(first, False)
        over = sum(
            n_block - (mine + 1 if pair == first else bound(first, pair)) for pair in fed(first)
        )
        pl.when(over > 0)(lambda: pl.semaphore_wait(ready, over))
        send(first, True)
        count_load.wait()
        odd = first % 2 == 1
        stop = n_pair if odd else first + 2
        lane = lax.broadcasted_iota(jnp.int32, (1, LANES), 1)
        pieces = []
        for slot in range(0, n_block, 2):
            bases = []
            for one in (slot, slot + 1):
                row, col = place(one)
                bases.append((row * n_col + col) * tile)
            pieces.append(jnp.where(lane < tile, bases[0] + lane, bases[1] + lane - tile))
        index = jnp.concatenate(pieces, axis=1)
        valid = {time: index < counts_ref[time] for time in range(first, stop + 1)}
        numbers = {time: counts_ref[time].astype(jnp.float32) for time in range(first, stop + 1)}
        lefts, rights, extras, totals = {}, {}, {}, {}

        def arrive(part):
            for time in range(first, stop + 1):
                start, end = parts[part]
                if part == 0 and (time == first or (odd and time == n_pair)):
                    start = 1
                arrival(blocks(time, start, end - start), x_recv.at[time, part]).wait_recv()
                if odd and time < first + 2:
                    relay(time, part).start()

        def prepare(part):
            start, end = parts[part]
            width = (end - start) * tile
            lanes = slice(start * tile, end * tile)
            feature = lax.broadcasted_iota(jnp.int32, (PIECES, width), 0)
            for time in range(first, stop + 1):
                z = unpacked(xg, time * n_block + start, time * n_block + end)
                extras[time, part] = z[pca : pca + 1]
                z = jnp.where(feature < pca, z, 0.0)
                norm = jnp.sum(z * z, axis=0, keepdims=True) * LOG2E
                if time < stop:
                    a = jnp.where(
                        feature < pca, z * (2.0 * LOG2E), jnp.where(feature == pca, -norm, 1.0)
                    )
                    a1, a2, a3 = split3(a)
                    rights[time, part] = jnp.concatenate([a1, a2, a1, a2, a3, a1], axis=0)
                if time > first:
                    low = jnp.where(valid[time][:, lanes], -norm, -BIG)
                    b = jnp.where(feature < pca, z, jnp.where(feature == pca, 1.0, low))
                    b1, b2, b3 = split3(b)
                    lefts[time, part] = jnp.concatenate([b1, b1, b2, b2, b1, b3], axis=0)

        def fill(pair, part, other):
            first_row, first_lane = parts[part][0] * tile, parts[other][0] * tile
            left, right = lefts[pair + 1, part], rights[pair, other]
            lanes = slice(first_lane, first_lane + right.shape[1])
            total = totals.get((pair, other), jnp.zeros((8, right.shape[1]), jnp.float32))
            for j in range(left.shape[1] // LANES):
                values = jnp.exp2(dot(left[:, j * LANES : (j + 1) * LANES], right, ((0,), (0,))))
                for k in range(LANES // 8):
                    total = total + values[k * 8 : (k + 1) * 8]
                rows = slice(first_row + j * LANES, first_row + (j + 1) * LANES)
                kernel[pair, rows, lanes] = values
            totals[pair, other] = total

        def extra(time):
            return jnp.concatenate([extras[time, 0], extras[time, 1]], axis=1)

        scale_u, row_totals = {}, {}
        iota_rows = lax.broadcasted_iota(jnp.int32, (tile, 1), 0)

        def settle(pairs):
            for pair in pairs:
                total = jnp.concatenate([totals[pair, 0], totals[pair, 1]], axis=1)
                total = jnp.sum(total, axis=0, keepdims=True)
                share = jnp.sqrt(extra(pair) / numbers[pair])
                scale_u[pair] = jnp.where(valid[pair], share * lax.rsqrt(total), 0.0)
            sums = {pair: jnp.zeros((8, cells), jnp.float32) for pair in pairs}
            for slot in range(n_block):
                rows = slice(slot * tile, (slot + 1) * tile)
                row, col = place(slot)
                position = (row * n_col + col) * tile + iota_rows
                for pair in pairs:
                    values = kernel[pair, rows, :]
                    terms = values * scale_u[pair]
                    folded = terms[:, :LANES]
                    for j in range(1, cells // LANES):
                        folded = folded + terms[:, j * LANES : (j + 1) * LANES]
                    column = jnp.sum(folded, axis=1, keepdims=True)
                    is_target = position < counts_ref[pair + 1]
                    column = jnp.where(is_target, column, 1.0)
                    power = jnp.log2(column) + jnp.log2(jnp.full((tile, 1), numbers[pair + 1]))
                    scale_v = jnp.where(is_target, jnp.exp2(-target_power * power), 0.0)
                    scaled = values * scale_v
                    for k in range(tile // 8):
                        sums[pair] = sums[pair] + scaled[k * 8 : (k + 1) * 8]
                    high, low = split2(scaled)
                    k1[pair, rows, :] = high
                    k2[pair, rows, :] = low
            for pair in pairs:
                row_totals[pair] = jnp.sum(sums[pair], axis=0, keepdims=True)

        def advance(pair, fates):
            width = cells if pair > first else LANES
            share = jnp.where(valid[pair], 1.0 / row_totals[pair], 0.0)
            f1, f2 = split2(fates)
            high, low = k1[pair, :, :width], k2[pair, :, :width]
            sums = dot(jnp.concatenate([f1, f2], axis=0), high, ((1,), (0,)))
            sums = sums[:CLASSES] + sums[CLASSES:] + dot(f1, low, ((1,), (0,)))
            return sums * share[:, :width]

        alone = odd and first + 1 < n_pair
        lead = range(stop - 1, first if alone else first - 1, -1)
        arrive(0)
        prepare(0)
        for pair in lead:
            fill(pair, 0, 0)
        arrive(1)
        prepare(1)
        for pair in lead:
            fill(pair, 0, 1)
            fill(pair, 1, 0)
            fill(pair, 1, 1)
        settle(lead)
        if stop == n_pair:
            classes = lax.broadcasted_iota(jnp.int32, (CLASSES, cells), 0).astype(jnp.float32)
            fates = jnp.where((extra(n_pair) == classes) & valid[n_pair], 1.0, 0.0)
        else:
            f_copy.wait_recv()
            fates = fin[...]
        for pair in range(stop - 1, first, -1):
            fates = advance(pair, fates)
        if alone:
            fout[...] = fates
            f_copy.start()
            for part in range(2):
                for other in range(2):
                    fill(first, part, other)
            settle([first])
        fates = advance(first, fates)
        mass = jnp.where(
            valid[first], numbers[first] * scale_u[first] * row_totals[first], 0.0
        )
        fates_ref[0] = fates[:, :tile]
        mass_ref[...] = mass[:, :tile]
        if odd:
            arrival(blocks(first, 0, 2 * n_block), x_recv.at[0, 0], r_send).wait_send()
            if alone:
                f_copy.wait_send()
        number = len(fed(first)) * n_block - 1 + (n_block - 1) * odd
        arrival(blocks(0, 0, number), x_recv.at[0, 0]).wait_send()

    for pair in range(n_pair):

        @pl.when(pair_at == pair)
        def _(pair=pair):
            body(pair)


def written(fates_ref, mass_ref, fates_out, mass_out, sems):
    copies = (
        pltpu.make_async_copy(mass_ref, mass_out, sems.at[0]),
        pltpu.make_async_copy(fates_ref, fates_out, sems.at[1]),
    )
    for copy in copies:
        copy.start()
    for copy in copies:
        copy.wait()


def per_device_fused(coords, final_coords, growth, counts, labels):
    pca, tile = coords.shape[1], coords.shape[2]
    n_pair = lax.axis_size("pair")
    n_row = lax.axis_size("row")
    n_col = lax.axis_size("col")
    n_block = n_row * n_col
    cells = n_block * tile
    vmem = pl.BlockSpec(memory_space=pltpu.VMEM)
    dma = pltpu.SemaphoreType.DMA
    fates, mass = pl.pallas_call(
        functools.partial(fused, (n_pair, n_row, n_col, tile)),
        out_shape=(
            pltpu.VMEM((1, CLASSES, tile), jnp.float32),
            pltpu.VMEM((1, tile), jnp.float32),
        ),
        in_specs=[pl.BlockSpec(memory_space=pl.ANY)] * 5,
        out_specs=(vmem, vmem),
        scratch_shapes=[
            pltpu.SMEM((n_pair + 1,), jnp.int32),
            pltpu.VMEM((pca, 1, tile), jnp.float32),
            pltpu.VMEM((pca, tile), jnp.float32),
            pltpu.VMEM((1, tile), jnp.float32),
            pltpu.VMEM((1, tile), jnp.int32),
            pltpu.VMEM(((n_pair + 1) * n_block, HALF, LANES), jnp.float32),
            pltpu.VMEM((n_pair, cells, cells), jnp.float32),
            pltpu.VMEM((n_pair, cells, cells), jnp.bfloat16),
            pltpu.VMEM((n_pair, cells, cells), jnp.bfloat16),
            pltpu.VMEM((CLASSES, cells), jnp.float32),
            pltpu.VMEM((CLASSES, cells), jnp.float32),
            dma((5,)),
            dma,
            dma,
            dma((n_pair + 1, 2)),
            dma,
            dma,
            pltpu.SemaphoreType.REGULAR,
        ],
        compiler_params=pltpu.CompilerParams(collective_id=0, has_side_effects=True),
    )(counts, jnp.transpose(coords, (1, 0, 2)), final_coords, growth, labels[None, :])
    return pl.pallas_call(
        written,
        out_shape=(
            jax.ShapeDtypeStruct(fates.shape, jnp.float32),
            jax.ShapeDtypeStruct(mass.shape, jnp.float32),
        ),
        in_specs=(vmem, vmem),
        out_specs=(pl.BlockSpec(memory_space=pl.ANY), pl.BlockSpec(memory_space=pl.ANY)),
        scratch_shapes=[dma((2,))],
    )(*(pltpu.with_memory_space_constraint(array, pltpu.VMEM) for array in (fates, mass)))


def solution(mesh):
    placed = (
        P("pair", None, ("row", "col")),
        P(None, ("row", "col")),
        P("pair", ("row", "col")),
        P(),
        P(("row", "col")),
    )
    out = (P("pair", None, ("row", "col")), P("pair", ("row", "col")))

    def whole(coords, final_coords, growth, counts, labels):
        cells = coords.shape[2]
        pairs = mesh.shape["pair"]
        blocks = mesh.shape["row"] * mesh.shape["col"]
        fits = (
            2 * cells == LANES * blocks
            and mesh.shape["row"] % 2 == 0
            and mesh.shape["col"] > 1
            and pairs % 2 == 0
            and coords.shape[0] == pairs
            and coords.shape[1] + 2 <= PIECES
            and 8 * pairs * cells * cells <= FUSED_BYTES
        )
        body = per_device_fused if fits else per_device
        return jax.shard_map(
            body, mesh=mesh, in_specs=placed, out_specs=out, check_vma=False
        )(coords, final_coords, growth, counts, labels)

    return whole
```

```python
import functools
import jax
import jax.numpy as jnp
from jax import lax
from jax.experimental import pallas as pl
from jax.experimental.pallas import tpu as pltpu
from jax.sharding import PartitionSpec as P

CLASSES = 16
FUSED_BYTES = 16 * 1024 * 1024


cost_scale = 1.0
source_power = 0.5
target_power = 50.0 / 51.0


def shifted_2(block, axis, distance):
    devices = range(lax.axis_size(axis))
    route = [(i - distance, i) for i in devices if i - distance in devices]
    return lax.ppermute(block, axis, route)


def kernel_tile(sources, targets):
    cross = lax.dot_general(
        sources,
        targets,
        (((0,), (0,)), ((), ())),
        precision=lax.Precision.HIGHEST,
        preferred_element_type=jnp.float32,
    )
    source_norms = jnp.sum(sources * sources, axis=0)
    target_norms = jnp.sum(targets * targets, axis=0)
    return jnp.exp(-(source_norms[:, None] + target_norms[None, :] - 2.0 * cross) / cost_scale)


def forward(kernel, weights):
    return lax.dot_general(
        weights,
        kernel,
        (((1,), (1,)), ((), ())),
        precision=lax.Precision.HIGHEST,
        preferred_element_type=jnp.float32,
    )


def backward(kernel, scales):
    return jnp.dot(
        scales, kernel, precision=lax.Precision.HIGHEST, preferred_element_type=jnp.float32
    )


def per_device(coords, final_coords, growth, counts, labels):
    tile = coords.shape[2]
    n_pair = lax.axis_size("pair")
    n_row = lax.axis_size("row")
    n_col = lax.axis_size("col")
    pair_at = lax.axis_index("pair")
    row_at = lax.axis_index("row")
    col_at = lax.axis_index("col")
    source_count = n_col * tile
    target_count = n_row * tile
    own_coords = coords[0]
    sources, source_growth = (
        lax.all_gather(own_coords, "col", axis=1, tiled=True),
        lax.all_gather(growth[0], "col", axis=0, tiled=True),
    )
    shifted = shifted_2(own_coords, "pair", -1)
    is_last = pair_at == n_pair - 1
    own_targets = jnp.where(is_last, final_coords, shifted)
    label_values = labels.astype(jnp.float32)
    position = lax.iota(jnp.int32, target_count)
    targets, target_labels = (
        lax.all_gather(own_targets, "row", axis=1, tiled=True),
        lax.all_gather(label_values, "row", axis=0, tiled=True),
    )
    target_index = position // tile * (n_col * tile) + col_at * tile + position % tile

    def hand_over(fates_now):
        incoming = shifted_2(fates_now, "pair", -1)
        return lax.all_gather(incoming, "row", axis=1, tiled=True)

    source_number = counts[pair_at]
    target_number = counts[pair_at + 1]
    source_total = source_number.astype(jnp.float32)
    target_total = target_number.astype(jnp.float32)
    source_index = row_at * source_count + lax.iota(jnp.int32, source_count)
    source_valid = source_index < source_number
    target_valid = target_index < target_number
    kernel = kernel_tile(sources, targets)
    start_terms = forward(kernel, target_valid.astype(jnp.float32)[None, :])[0]
    start_rows = lax.psum(start_terms, "col")
    source_mass = jnp.where(source_valid, source_growth / source_total, 0.0)
    scale_u = jnp.where(source_valid, jnp.power(source_mass / start_rows, source_power), 0.0)
    column_terms = backward(kernel, scale_u)
    column_totals = lax.psum(column_terms, "row")
    target_mass = target_valid.astype(jnp.float32) / target_total
    scale_v = jnp.where(target_valid, jnp.power(target_mass / column_totals, target_power), 0.0)
    own_offset = col_at * tile
    own_valid = lax.dynamic_slice_in_dim(source_valid, own_offset, tile, 0)
    own_scale = lax.dynamic_slice_in_dim(scale_u, own_offset, tile, 0)
    class_values = lax.iota(jnp.int32, CLASSES).astype(jnp.float32)
    label_table = jnp.where(
        (target_labels[None, :] == class_values[:, None]) & target_valid[None, :], 1.0, 0.0
    ).astype(jnp.float32)
    empty = jnp.zeros((CLASSES, tile), jnp.float32)
    final_terms = forward(kernel, scale_v[None, :])[0]
    final_rows = lax.psum(final_terms, "col")
    own_rows = lax.dynamic_slice_in_dim(final_rows, own_offset, tile, 0)
    safe_rows = jnp.where(own_valid, own_rows, 1.0)

    def advance(turn, fates_now):
        carried = jnp.where(is_last, label_table, hand_over(fates_now))
        terms = forward(kernel, carried * scale_v[None, :])
        sums = lax.psum_scatter(terms, "col", scatter_dimension=1, tiled=True)
        return jnp.where(own_valid[None, :], sums / safe_rows[None, :], 0.0)

    fates = lax.fori_loop(0, n_pair, advance, empty)
    mass = jnp.where(own_valid, source_total * own_scale * own_rows, 0.0)
    return (fates[None], mass[None])


LANES = 128
PIECES = 32
HALF = 16
BIG = 1e30
LOG2E = 1.4426950408889634
MESH = pl.DeviceIdType.MESH


def split3(a):
    first = a.astype(jnp.bfloat16)
    rest = a - first.astype(jnp.float32)
    second = rest.astype(jnp.bfloat16)
    third = (rest - second.astype(jnp.float32)).astype(jnp.bfloat16)
    return first, second, third


def split2(a):
    first = a.astype(jnp.bfloat16)
    return first, (a - first.astype(jnp.float32)).astype(jnp.bfloat16)


def dot(a, b, dims):
    return lax.dot_general(a, b, (dims, ((), ())), preferred_element_type=jnp.float32)


def packed(block, extra):
    low = block[:HALF]
    rest = block.shape[0] - HALF
    fill = jnp.zeros((HALF - rest - 1, block.shape[1]), jnp.float32)
    high = jnp.concatenate([block[HALF:], extra, fill], axis=0)
    return jnp.concatenate([low, high], axis=1)


def unpacked(ref, start, stop):
    lows, highs = [], []
    lane = lax.broadcasted_iota(jnp.int32, (HALF, LANES), 1)
    for slot in range(start, stop, 2):
        a, b = ref[slot], ref[slot + 1]
        swap_a, swap_b = pltpu.roll(a, LANES // 2, 1), pltpu.roll(b, LANES // 2, 1)
        lows.append(jnp.where(lane < LANES // 2, a, swap_b))
        highs.append(jnp.where(lane < LANES // 2, swap_a, b))
    low, high = jnp.concatenate(lows, axis=1), jnp.concatenate(highs, axis=1)
    return jnp.concatenate([low, high], axis=0)


def fused(
    sizes,
    counts_in,
    coords_in,
    final_in,
    growth_in,
    labels_in,
    fates_ref,
    mass_ref,
    counts_ref,
    coords_ref,
    final_ref,
    growth_ref,
    labels_ref,
    xg,
    kernel,
    k1,
    k2,
    fin,
    fout,
    own_sems,
    x_send,
    x_recv,
    f_recv,
    ready,
):
    n_pair, n_row, n_col, tile = sizes
    n_block = n_row * n_col
    near = n_block - n_row
    cells = n_block * tile
    pca = coords_in.shape[0]
    pair_at = lax.axis_index("pair")
    row_at = lax.axis_index("row")
    col_at = lax.axis_index("col")

    def place(slot):
        along, down = divmod(slot, n_row)
        return (row_at + down) % n_row, (col_at + along) % n_col

    barrier = pltpu.get_barrier_semaphore()
    mine = col_at * n_row + row_at

    def fed(pair):
        return [other for other in range(pair + 1) if other == pair or other % 2]

    def feeding(pair):
        return [other for other in range(n_pair) if pair in fed(other)]

    def met(pair):
        return [other for other in range(n_pair) if other in fed(pair) + feeding(pair)]

    def at(block):
        return block % n_row, block // n_row

    def signal(semaphore, pair, block):
        pl.semaphore_signal(
            semaphore, inc=1, device_id=(pair, *at(block)), device_id_type=MESH
        )

    def loop(start, stop, act):
        def step(block, carry):
            act(block)
            return carry

        lax.fori_loop(start, stop, step, 0)

    count_load = pltpu.make_async_copy(counts_in, counts_ref, own_sems.at[4])
    own_loads = (
        pltpu.make_async_copy(coords_in, coords_ref, own_sems.at[0]),
        pltpu.make_async_copy(growth_in, growth_ref, own_sems.at[1]),
        pltpu.make_async_copy(final_in, final_ref, own_sems.at[2]),
        pltpu.make_async_copy(labels_in, labels_ref, own_sems.at[3]),
    )
    for load in own_loads:
        load.start()
    count_load.start()

    def block_copy(time, pair, block):
        row, col = at(block)
        there = (col_at - col) % n_col * n_row + (row_at - row) % n_row
        return pltpu.make_async_remote_copy(
            src_ref=xg.at[time * n_block],
            dst_ref=xg.at[time * n_block + there],
            send_sem=x_send,
            recv_sem=x_recv.at[time, there // near],
            device_id=(pair, row, col),
            device_id_type=MESH,
        )

    parts = ((0, near), (near, n_block))
    below = jnp.maximum(pair_at - 1, 0)

    def blocks(time, start, number):
        return xg.at[pl.ds(time * n_block + start, number)]

    def relay(time, part):
        start, stop = parts[part]
        block = blocks(time, start, stop - start)
        return pltpu.make_async_remote_copy(
            src_ref=block,
            dst_ref=block,
            send_sem=x_send,
            recv_sem=x_recv.at[time, part],
            device_id=(below, row_at, col_at),
            device_id_type=MESH,
        )

    f_copy = pltpu.make_async_remote_copy(
        src_ref=fout,
        dst_ref=fin,
        send_sem=x_send,
        recv_sem=f_recv,
        device_id=(below, row_at, col_at),
        device_id_type=MESH,
    )

    def arrival(buffer, sem):
        return pltpu.make_async_remote_copy(
            src_ref=buffer,
            dst_ref=buffer,
            send_sem=x_send,
            recv_sem=sem,
            device_id=(pair_at, row_at, col_at),
            device_id_type=MESH,
        )

    def bound(own, pair):
        shift = 4 * n_row * (own // 2 - pair // 2) + (pair < own)
        return jnp.minimum(jnp.maximum(mine + shift, 0), n_block)

    def inner(block):
        row, col = at(block)
        return (row > 0 and col > 0, -row - col, row)

    order = sorted(range(1, n_block), key=inner)

    def send(own, is_late):
        for pair in fed(own):

            def step(block, pair=pair):
                block_copy(own, pair, block).start()
                if pair == own and own % 2:
                    block_copy(n_pair, pair, block).start()

            if not is_late:
                pl.when((mine if pair == own else bound(own, pair)) > 0)(lambda: step(0))
                continue
            if pair < own:
                pl.when(bound(own, pair) == 0)(lambda: step(0))
            for block in order:
                if pair < own:
                    step(block)
                else:
                    pl.when(mine != block)(functools.partial(step, block))

    def body(first):
        for pair in met(first):
            start = mine + 1 if pair == first else bound(first, pair)
            loop(start, n_block, functools.partial(signal, barrier, pair))
        if first % 2 == 0:
            signal(barrier, first + 1, mine)
        under = sum(mine if pair == first else bound(first, pair) for pair in met(first))
        if first % 2:
            pl.semaphore_wait(barrier, under + 1)
        else:
            pl.when(under > 0)(lambda: pl.semaphore_wait(barrier, under))
        for pair in feeding(first):
            stop = mine if pair == first else bound(first, pair)
            loop(0, stop, functools.partial(signal, ready, pair))
        for load in own_loads:
            load.wait()
        xg[first * n_block] = packed(coords_ref[:, 0, :], growth_ref[...])
        if first % 2:
            xg[n_pair * n_block] = packed(final_ref[...], labels_ref[...].astype(jnp.float32))
        send(first, False)
        over = sum(
            n_block - (mine + 1 if pair == first else bound(first, pair)) for pair in fed(first)
        )
        pl.when(over > 0)(lambda: pl.semaphore_wait(ready, over))
        send(first, True)
        count_load.wait()
        odd = first % 2 == 1
        stop = n_pair if odd else first + 2
        lane = lax.broadcasted_iota(jnp.int32, (1, LANES), 1)
        pieces = []
        for slot in range(0, n_block, 2):
            bases = []
            for one in (slot, slot + 1):
                row, col = place(one)
                bases.append((row * n_col + col) * tile)
            pieces.append(jnp.where(lane < tile, bases[0] + lane, bases[1] + lane - tile))
        index = jnp.concatenate(pieces, axis=1)
        valid = {time: index < counts_ref[time] for time in range(first, stop + 1)}
        numbers = {time: counts_ref[time].astype(jnp.float32) for time in range(first, stop + 1)}
        lefts, rights, extras, totals = {}, {}, {}, {}

        def arrive(part):
            for time in range(first, stop + 1):
                start, end = parts[part]
                if part == 0 and (time == first or (odd and time == n_pair)):
                    start = 1
                arrival(blocks(time, start, end - start), x_recv.at[time, part]).wait_recv()
                if odd and time < first + 2:
                    relay(time, part).start()

        def prepare(part):
            start, end = parts[part]
            width = (end - start) * tile
            lanes = slice(start * tile, end * tile)
            feature = lax.broadcasted_iota(jnp.int32, (PIECES, width), 0)
            for time in range(first, stop + 1):
                z = unpacked(xg, time * n_block + start, time * n_block + end)
                extras[time, part] = z[pca : pca + 1]
                z = jnp.where(feature < pca, z, 0.0)
                norm = jnp.sum(z * z, axis=0, keepdims=True) * LOG2E
                if time < stop:
                    a = jnp.where(
                        feature < pca, z * (2.0 * LOG2E), jnp.where(feature == pca, -norm, 1.0)
                    )
                    a1, a2, a3 = split3(a)
                    rights[time, part] = jnp.concatenate([a1, a2, a1, a2, a3, a1], axis=0)
                if time > first:
                    low = jnp.where(valid[time][:, lanes], -norm, -BIG)
                    b = jnp.where(feature < pca, z, jnp.where(feature == pca, 1.0, low))
                    b1, b2, b3 = split3(b)
                    lefts[time, part] = jnp.concatenate([b1, b1, b2, b2, b1, b3], axis=0)

        def fill(pair, part, other):
            first_row, first_lane = parts[part][0] * tile, parts[other][0] * tile
            left, right = lefts[pair + 1, part], rights[pair, other]
            lanes = slice(first_lane, first_lane + right.shape[1])
            total = totals.get((pair, other), jnp.zeros((8, right.shape[1]), jnp.float32))
            for j in range(left.shape[1] // LANES):
                values = jnp.exp2(dot(left[:, j * LANES : (j + 1) * LANES], right, ((0,), (0,))))
                for k in range(LANES // 8):
                    total = total + values[k * 8 : (k + 1) * 8]
                rows = slice(first_row + j * LANES, first_row + (j + 1) * LANES)
                kernel[pair, rows, lanes] = values
            totals[pair, other] = total

        def extra(time):
            return jnp.concatenate([extras[time, 0], extras[time, 1]], axis=1)

        scale_u, row_totals = {}, {}
        iota_rows = lax.broadcasted_iota(jnp.int32, (tile, 1), 0)

        def settle(pairs):
            for pair in pairs:
                total = jnp.concatenate([totals[pair, 0], totals[pair, 1]], axis=1)
                total = jnp.sum(total, axis=0, keepdims=True)
                share = jnp.sqrt(extra(pair) / numbers[pair])
                scale_u[pair] = jnp.where(valid[pair], share * lax.rsqrt(total), 0.0)
            sums = {pair: jnp.zeros((8, cells), jnp.float32) for pair in pairs}
            for slot in range(n_block):
                rows = slice(slot * tile, (slot + 1) * tile)
                row, col = place(slot)
                position = (row * n_col + col) * tile + iota_rows
                for pair in pairs:
                    values = kernel[pair, rows, :]
                    terms = values * scale_u[pair]
                    folded = terms[:, :LANES]
                    for j in range(1, cells // LANES):
                        folded = folded + terms[:, j * LANES : (j + 1) * LANES]
                    column = jnp.sum(folded, axis=1, keepdims=True)
                    is_target = position < counts_ref[pair + 1]
                    column = jnp.where(is_target, column, 1.0)
                    power = jnp.log2(column) + jnp.log2(jnp.full((tile, 1), numbers[pair + 1]))
                    scale_v = jnp.where(is_target, jnp.exp2(-target_power * power), 0.0)
                    scaled = values * scale_v
                    for k in range(tile // 8):
                        sums[pair] = sums[pair] + scaled[k * 8 : (k + 1) * 8]
                    high, low = split2(scaled)
                    k1[pair, rows, :] = high
                    k2[pair, rows, :] = low
            for pair in pairs:
                row_totals[pair] = jnp.sum(sums[pair], axis=0, keepdims=True)

        def advance(pair, fates):
            width = cells if pair > first else LANES
            share = jnp.where(valid[pair], 1.0 / row_totals[pair], 0.0)
            f1, f2 = split2(fates)
            high, low = k1[pair, :, :width], k2[pair, :, :width]
            if pair == n_pair - 1:
                sums = dot(f1, high, ((1,), (0,)))
            else:
                sums = dot(jnp.concatenate([f1, f2], axis=0), high, ((1,), (0,)))
                sums = sums[:CLASSES] + sums[CLASSES:]
            sums = sums + dot(f1, low, ((1,), (0,)))
            return sums * share[:, :width]

        alone = odd and first + 1 < n_pair
        lead = range(stop - 1, first if alone else first - 1, -1)
        arrive(0)
        prepare(0)
        for pair in lead:
            fill(pair, 0, 0)
        arrive(1)
        prepare(1)
        for pair in lead:
            fill(pair, 0, 1)
            fill(pair, 1, 0)
            fill(pair, 1, 1)
        settle(lead)
        if stop == n_pair:
            classes = lax.broadcasted_iota(jnp.int32, (CLASSES, cells), 0).astype(jnp.float32)
            fates = jnp.where((extra(n_pair) == classes) & valid[n_pair], 1.0, 0.0)
        else:
            f_copy.wait_recv()
            fates = fin[...]
        for pair in range(stop - 1, first, -1):
            fates = advance(pair, fates)
        if alone:
            fout[...] = fates
            f_copy.start()
            for part in range(2):
                for other in range(2):
                    fill(first, part, other)
            settle([first])
        fates = advance(first, fates)
        mass = jnp.where(
            valid[first], numbers[first] * scale_u[first] * row_totals[first], 0.0
        )
        fates_ref[0] = fates[:, :tile]
        mass_ref[...] = mass[:, :tile]
        number = len(fed(first)) * n_block - 1 + (n_block - 1) * odd
        if odd:
            number = number + 2 * n_block
            if alone:
                f_copy.wait_send()
        arrival(blocks(0, 0, number), x_recv.at[0, 0]).wait_send()

    for pair in range(n_pair):

        @pl.when(pair_at == pair)
        def _(pair=pair):
            body(pair)


def written(fates_ref, mass_ref, fates_out, mass_out, sems):
    copies = (
        pltpu.make_async_copy(mass_ref, mass_out, sems.at[0]),
        pltpu.make_async_copy(fates_ref, fates_out, sems.at[1]),
    )
    for copy in copies:
        copy.start()
    for copy in copies:
        copy.wait()


def per_device_fused(coords, final_coords, growth, counts, labels):
    pca, tile = coords.shape[1], coords.shape[2]
    n_pair = lax.axis_size("pair")
    n_row = lax.axis_size("row")
    n_col = lax.axis_size("col")
    n_block = n_row * n_col
    cells = n_block * tile
    vmem = pl.BlockSpec(memory_space=pltpu.VMEM)
    dma = pltpu.SemaphoreType.DMA
    fates, mass = pl.pallas_call(
        functools.partial(fused, (n_pair, n_row, n_col, tile)),
        out_shape=(
            pltpu.VMEM((1, CLASSES, tile), jnp.float32),
            pltpu.VMEM((1, tile), jnp.float32),
        ),
        in_specs=[pl.BlockSpec(memory_space=pl.ANY)] * 5,
        out_specs=(vmem, vmem),
        scratch_shapes=[
            pltpu.SMEM((n_pair + 1,), jnp.int32),
            pltpu.VMEM((pca, 1, tile), jnp.float32),
            pltpu.VMEM((pca, tile), jnp.float32),
            pltpu.VMEM((1, tile), jnp.float32),
            pltpu.VMEM((1, tile), jnp.int32),
            pltpu.VMEM(((n_pair + 1) * n_block, HALF, LANES), jnp.float32),
            pltpu.VMEM((n_pair, cells, cells), jnp.float32),
            pltpu.VMEM((n_pair, cells, cells), jnp.bfloat16),
            pltpu.VMEM((n_pair, cells, cells), jnp.bfloat16),
            pltpu.VMEM((CLASSES, cells), jnp.float32),
            pltpu.VMEM((CLASSES, cells), jnp.float32),
            dma((5,)),
            dma,
            dma((n_pair + 1, 2)),
            dma,
            pltpu.SemaphoreType.REGULAR,
        ],
        compiler_params=pltpu.CompilerParams(collective_id=0, has_side_effects=True),
    )(counts, jnp.transpose(coords, (1, 0, 2)), final_coords, growth, labels[None, :])
    return pl.pallas_call(
        written,
        out_shape=(
            jax.ShapeDtypeStruct(fates.shape, jnp.float32),
            jax.ShapeDtypeStruct(mass.shape, jnp.float32),
        ),
        in_specs=(vmem, vmem),
        out_specs=(pl.BlockSpec(memory_space=pl.ANY), pl.BlockSpec(memory_space=pl.ANY)),
        scratch_shapes=[dma((2,))],
    )(*(pltpu.with_memory_space_constraint(array, pltpu.VMEM) for array in (fates, mass)))


def solution(mesh):
    placed = (
        P("pair", None, ("row", "col")),
        P(None, ("row", "col")),
        P("pair", ("row", "col")),
        P(),
        P(("row", "col")),
    )
    out = (P("pair", None, ("row", "col")), P("pair", ("row", "col")))

    def whole(coords, final_coords, growth, counts, labels):
        cells = coords.shape[2]
        pairs = mesh.shape["pair"]
        blocks = mesh.shape["row"] * mesh.shape["col"]
        fits = (
            2 * cells == LANES * blocks
            and mesh.shape["row"] % 2 == 0
            and mesh.shape["col"] > 1
            and pairs % 2 == 0
            and coords.shape[0] == pairs
            and coords.shape[1] + 2 <= PIECES
            and 8 * pairs * cells * cells <= FUSED_BYTES
        )
        body = per_device_fused if fits else per_device
        return jax.shard_map(
            body, mesh=mesh, in_specs=placed, out_specs=out, check_vma=False
        )(coords, final_coords, growth, counts, labels)

    return whole
```

```python
import functools
import jax
import jax.numpy as jnp
from jax import lax
from jax.experimental import pallas as pl
from jax.experimental.pallas import tpu as pltpu
from jax.sharding import PartitionSpec as P

CLASSES = 16
FUSED_BYTES = 16 * 1024 * 1024


cost_scale = 1.0
source_power = 0.5
target_power = 50.0 / 51.0


def shifted_2(block, axis, distance):
    devices = range(lax.axis_size(axis))
    route = [(i - distance, i) for i in devices if i - distance in devices]
    return lax.ppermute(block, axis, route)


def kernel_tile(sources, targets):
    cross = lax.dot_general(
        sources,
        targets,
        (((0,), (0,)), ((), ())),
        precision=lax.Precision.HIGHEST,
        preferred_element_type=jnp.float32,
    )
    source_norms = jnp.sum(sources * sources, axis=0)
    target_norms = jnp.sum(targets * targets, axis=0)
    return jnp.exp(-(source_norms[:, None] + target_norms[None, :] - 2.0 * cross) / cost_scale)


def forward(kernel, weights):
    return lax.dot_general(
        weights,
        kernel,
        (((1,), (1,)), ((), ())),
        precision=lax.Precision.HIGHEST,
        preferred_element_type=jnp.float32,
    )


def backward(kernel, scales):
    return jnp.dot(
        scales, kernel, precision=lax.Precision.HIGHEST, preferred_element_type=jnp.float32
    )


def per_device(coords, final_coords, growth, counts, labels):
    tile = coords.shape[2]
    n_pair = lax.axis_size("pair")
    n_row = lax.axis_size("row")
    n_col = lax.axis_size("col")
    pair_at = lax.axis_index("pair")
    row_at = lax.axis_index("row")
    col_at = lax.axis_index("col")
    source_count = n_col * tile
    target_count = n_row * tile
    own_coords = coords[0]
    sources, source_growth = (
        lax.all_gather(own_coords, "col", axis=1, tiled=True),
        lax.all_gather(growth[0], "col", axis=0, tiled=True),
    )
    shifted = shifted_2(own_coords, "pair", -1)
    is_last = pair_at == n_pair - 1
    own_targets = jnp.where(is_last, final_coords, shifted)
    label_values = labels.astype(jnp.float32)
    position = lax.iota(jnp.int32, target_count)
    targets, target_labels = (
        lax.all_gather(own_targets, "row", axis=1, tiled=True),
        lax.all_gather(label_values, "row", axis=0, tiled=True),
    )
    target_index = position // tile * (n_col * tile) + col_at * tile + position % tile

    def hand_over(fates_now):
        incoming = shifted_2(fates_now, "pair", -1)
        return lax.all_gather(incoming, "row", axis=1, tiled=True)

    source_number = counts[pair_at]
    target_number = counts[pair_at + 1]
    source_total = source_number.astype(jnp.float32)
    target_total = target_number.astype(jnp.float32)
    source_index = row_at * source_count + lax.iota(jnp.int32, source_count)
    source_valid = source_index < source_number
    target_valid = target_index < target_number
    kernel = kernel_tile(sources, targets)
    start_terms = forward(kernel, target_valid.astype(jnp.float32)[None, :])[0]
    start_rows = lax.psum(start_terms, "col")
    source_mass = jnp.where(source_valid, source_growth / source_total, 0.0)
    scale_u = jnp.where(source_valid, jnp.power(source_mass / start_rows, source_power), 0.0)
    column_terms = backward(kernel, scale_u)
    column_totals = lax.psum(column_terms, "row")
    target_mass = target_valid.astype(jnp.float32) / target_total
    scale_v = jnp.where(target_valid, jnp.power(target_mass / column_totals, target_power), 0.0)
    own_offset = col_at * tile
    own_valid = lax.dynamic_slice_in_dim(source_valid, own_offset, tile, 0)
    own_scale = lax.dynamic_slice_in_dim(scale_u, own_offset, tile, 0)
    class_values = lax.iota(jnp.int32, CLASSES).astype(jnp.float32)
    label_table = jnp.where(
        (target_labels[None, :] == class_values[:, None]) & target_valid[None, :], 1.0, 0.0
    ).astype(jnp.float32)
    empty = jnp.zeros((CLASSES, tile), jnp.float32)
    final_terms = forward(kernel, scale_v[None, :])[0]
    final_rows = lax.psum(final_terms, "col")
    own_rows = lax.dynamic_slice_in_dim(final_rows, own_offset, tile, 0)
    safe_rows = jnp.where(own_valid, own_rows, 1.0)

    def advance(turn, fates_now):
        carried = jnp.where(is_last, label_table, hand_over(fates_now))
        terms = forward(kernel, carried * scale_v[None, :])
        sums = lax.psum_scatter(terms, "col", scatter_dimension=1, tiled=True)
        return jnp.where(own_valid[None, :], sums / safe_rows[None, :], 0.0)

    fates = lax.fori_loop(0, n_pair, advance, empty)
    mass = jnp.where(own_valid, source_total * own_scale * own_rows, 0.0)
    return (fates[None], mass[None])


LANES = 128
PIECES = 32
HALF = 16
BIG = 1e30
LOG2E = 1.4426950408889634
MESH = pl.DeviceIdType.MESH


def split3(a):
    first = a.astype(jnp.bfloat16)
    rest = a - first.astype(jnp.float32)
    second = rest.astype(jnp.bfloat16)
    third = (rest - second.astype(jnp.float32)).astype(jnp.bfloat16)
    return first, second, third


def split2(a):
    first = a.astype(jnp.bfloat16)
    return first, (a - first.astype(jnp.float32)).astype(jnp.bfloat16)


def dot(a, b, dims):
    return lax.dot_general(a, b, (dims, ((), ())), preferred_element_type=jnp.float32)


def packed(block, extra):
    low = block[:HALF]
    rest = block.shape[0] - HALF
    fill = jnp.zeros((HALF - rest - 1, block.shape[1]), jnp.float32)
    high = jnp.concatenate([block[HALF:], extra, fill], axis=0)
    return jnp.concatenate([low, high], axis=1)


def unpacked(ref, start, stop):
    lows, highs = [], []
    lane = lax.broadcasted_iota(jnp.int32, (HALF, LANES), 1)
    for slot in range(start, stop, 2):
        a, b = ref[slot], ref[slot + 1]
        swap_a, swap_b = pltpu.roll(a, LANES // 2, 1), pltpu.roll(b, LANES // 2, 1)
        lows.append(jnp.where(lane < LANES // 2, a, swap_b))
        highs.append(jnp.where(lane < LANES // 2, swap_a, b))
    low, high = jnp.concatenate(lows, axis=1), jnp.concatenate(highs, axis=1)
    return jnp.concatenate([low, high], axis=0)


def fused(
    sizes,
    counts_in,
    coords_in,
    final_in,
    growth_in,
    labels_in,
    fates_ref,
    mass_ref,
    counts_ref,
    coords_ref,
    final_ref,
    growth_ref,
    labels_ref,
    xg,
    kernel,
    k1,
    k2,
    fin,
    fout,
    results,
    own_sems,
    x_send,
    x_recv,
    f_recv,
    result_recv,
    ready,
):
    n_pair, n_row, n_col, tile = sizes
    n_block = n_row * n_col
    near = n_block - n_row
    cells = n_block * tile
    pca = coords_in.shape[0]
    pair_at = lax.axis_index("pair")
    row_at = lax.axis_index("row")
    col_at = lax.axis_index("col")

    def place(slot):
        along, down = divmod(slot, n_row)
        return (row_at + down) % n_row, (col_at + along) % n_col

    barrier = pltpu.get_barrier_semaphore()
    mine = col_at * n_row + row_at

    def at(block):
        return block % n_row, block // n_row

    def signal(semaphore, pair, block):
        pl.semaphore_signal(
            semaphore, inc=1, device_id=(pair, *at(block)), device_id_type=MESH
        )

    def loop(start, stop, act):
        def step(block, carry):
            act(block)
            return carry

        lax.fori_loop(start, stop, step, 0)

    count_load = pltpu.make_async_copy(counts_in, counts_ref, own_sems.at[4])
    own_loads = (
        pltpu.make_async_copy(coords_in, coords_ref, own_sems.at[0]),
        pltpu.make_async_copy(growth_in, growth_ref, own_sems.at[1]),
        pltpu.make_async_copy(final_in, final_ref, own_sems.at[2]),
        pltpu.make_async_copy(labels_in, labels_ref, own_sems.at[3]),
    )
    def block_copy(time, pair, block):
        row, col = at(block)
        there = (col_at - col) % n_col * n_row + (row_at - row) % n_row
        return pltpu.make_async_remote_copy(
            src_ref=xg.at[time * n_block],
            dst_ref=xg.at[time * n_block + there],
            send_sem=x_send,
            recv_sem=x_recv.at[time, there // near],
            device_id=(pair, row, col),
            device_id_type=MESH,
        )

    parts = ((0, near), (near, n_block))
    below = jnp.maximum(pair_at - 1, 0)

    def blocks(time, start, number):
        return xg.at[pl.ds(time * n_block + start, number)]

    def relay(time, part):
        start, stop = parts[part]
        block = blocks(time, start, stop - start)
        return pltpu.make_async_remote_copy(
            src_ref=block,
            dst_ref=block,
            send_sem=x_send,
            recv_sem=x_recv.at[time, part],
            device_id=(below, row_at, col_at),
            device_id_type=MESH,
        )

    f_copy = pltpu.make_async_remote_copy(
        src_ref=fout,
        dst_ref=fin,
        send_sem=x_send,
        recv_sem=f_recv,
        device_id=(below, row_at, col_at),
        device_id_type=MESH,
    )

    def arrival(buffer, sem):
        return pltpu.make_async_remote_copy(
            src_ref=buffer,
            dst_ref=buffer,
            send_sem=x_send,
            recv_sem=sem,
            device_id=(pair_at, row_at, col_at),
            device_id_type=MESH,
        )

    def inner(block):
        row, col = at(block)
        return (row > 0 and col > 0, -row - col, row)

    order = sorted(range(1, n_block), key=inner)

    def send(own, block):
        block_copy(own, min(own, 1), block).start()
        if own == 1:
            block_copy(n_pair, 1, block).start()

    def result_copy(pair):
        return pltpu.make_async_remote_copy(
            src_ref=results.at[pair],
            dst_ref=results.at[pair],
            send_sem=x_send,
            recv_sem=result_recv,
            device_id=(pair, row_at, col_at),
            device_id_type=MESH,
        )

    def only_send(first):
        for load in own_loads[:2]:
            load.start()
        for load in own_loads[:2]:
            load.wait()
        xg[first * n_block] = packed(coords_ref[:, 0, :], growth_ref[...])
        pl.semaphore_wait(barrier, n_block)
        for block in [0, *order]:
            send(first, block)
        arrival(results.at[first], result_recv).wait_recv()
        fates_ref[0] = results[first, :CLASSES, :tile]
        mass_ref[...] = results[first, CLASSES : CLASSES + 1, :tile]
        arrival(blocks(0, 0, n_block), x_recv.at[0, 0]).wait_send()

    def body(first):
        odd = first == 1
        stop = n_pair if odd else 2
        loads = (*own_loads[: 4 if odd else 2], count_load)
        for load in loads:
            load.start()
        if odd:
            for block in (*order, 0):
                for pair in range(2, n_pair):
                    signal(barrier, pair, block)
        else:
            signal(barrier, 1, mine)
        loop(mine + 1, n_block, functools.partial(signal, barrier, first))
        if odd:
            pl.semaphore_wait(barrier, mine + 1)
        else:
            pl.when(mine > 0)(lambda: pl.semaphore_wait(barrier, mine))
        loop(0, mine, functools.partial(signal, ready, first))
        for load in loads[:-1]:
            load.wait()
        xg[first * n_block] = packed(coords_ref[:, 0, :], growth_ref[...])
        if odd:
            xg[n_pair * n_block] = packed(final_ref[...], labels_ref[...].astype(jnp.float32))
        pl.when(mine > 0)(lambda: send(first, 0))
        over = n_block - 1 - mine
        pl.when(over > 0)(lambda: pl.semaphore_wait(ready, over))
        for block in order:
            pl.when(mine != block)(functools.partial(send, first, block))
        count_load.wait()
        lane = lax.broadcasted_iota(jnp.int32, (1, LANES), 1)
        pieces = []
        for slot in range(0, n_block, 2):
            bases = []
            for one in (slot, slot + 1):
                row, col = place(one)
                bases.append((row * n_col + col) * tile)
            pieces.append(jnp.where(lane < tile, bases[0] + lane, bases[1] + lane - tile))
        index = jnp.concatenate(pieces, axis=1)
        valid = {time: index < counts_ref[time] for time in range(first, stop + 1)}
        numbers = {time: counts_ref[time].astype(jnp.float32) for time in range(first, stop + 1)}
        lefts, rights, extras, totals = {}, {}, {}, {}

        def arrive(part):
            for time in range(first, stop + 1):
                start, end = parts[part]
                if part == 0 and (time == first or (odd and time == n_pair)):
                    start = 1
                arrival(blocks(time, start, end - start), x_recv.at[time, part]).wait_recv()
                if odd and time < first + 2:
                    relay(time, part).start()

        def prepare(part):
            start, end = parts[part]
            width = (end - start) * tile
            lanes = slice(start * tile, end * tile)
            feature = lax.broadcasted_iota(jnp.int32, (PIECES, width), 0)
            for time in range(first, stop + 1):
                z = unpacked(xg, time * n_block + start, time * n_block + end)
                extras[time, part] = z[pca : pca + 1]
                z = jnp.where(feature < pca, z, 0.0)
                norm = jnp.sum(z * z, axis=0, keepdims=True) * LOG2E
                if time < stop:
                    a = jnp.where(
                        feature < pca, z * (2.0 * LOG2E), jnp.where(feature == pca, -norm, 1.0)
                    )
                    a1, a2, a3 = split3(a)
                    rights[time, part] = jnp.concatenate([a1, a2, a1, a2, a3, a1], axis=0)
                if time > first:
                    low = jnp.where(valid[time][:, lanes], -norm, -BIG)
                    b = jnp.where(feature < pca, z, jnp.where(feature == pca, 1.0, low))
                    b1, b2, b3 = split3(b)
                    lefts[time, part] = jnp.concatenate([b1, b1, b2, b2, b1, b3], axis=0)

        def fill(pair, part, other):
            first_row, first_lane = parts[part][0] * tile, parts[other][0] * tile
            left, right = lefts[pair + 1, part], rights[pair, other]
            lanes = slice(first_lane, first_lane + right.shape[1])
            total = totals.get((pair, other), jnp.zeros((8, right.shape[1]), jnp.float32))
            for j in range(left.shape[1] // LANES):
                values = jnp.exp2(dot(left[:, j * LANES : (j + 1) * LANES], right, ((0,), (0,))))
                for k in range(LANES // 8):
                    total = total + values[k * 8 : (k + 1) * 8]
                rows = slice(first_row + j * LANES, first_row + (j + 1) * LANES)
                kernel[pair, rows, lanes] = values
            totals[pair, other] = total

        def extra(time):
            return jnp.concatenate([extras[time, 0], extras[time, 1]], axis=1)

        scale_u, row_totals = {}, {}
        iota_rows = lax.broadcasted_iota(jnp.int32, (tile, 1), 0)

        def settle(pairs):
            for pair in pairs:
                total = jnp.concatenate([totals[pair, 0], totals[pair, 1]], axis=1)
                total = jnp.sum(total, axis=0, keepdims=True)
                share = jnp.sqrt(extra(pair) / numbers[pair])
                scale_u[pair] = jnp.where(valid[pair], share * lax.rsqrt(total), 0.0)
            sums = {pair: jnp.zeros((8, cells), jnp.float32) for pair in pairs}
            for slot in range(n_block):
                rows = slice(slot * tile, (slot + 1) * tile)
                row, col = place(slot)
                position = (row * n_col + col) * tile + iota_rows
                for pair in pairs:
                    values = kernel[pair, rows, :]
                    terms = values * scale_u[pair]
                    folded = terms[:, :LANES]
                    for j in range(1, cells // LANES):
                        folded = folded + terms[:, j * LANES : (j + 1) * LANES]
                    column = jnp.sum(folded, axis=1, keepdims=True)
                    is_target = position < counts_ref[pair + 1]
                    column = jnp.where(is_target, column, 1.0)
                    power = jnp.log2(column) + jnp.log2(jnp.full((tile, 1), numbers[pair + 1]))
                    scale_v = jnp.where(is_target, jnp.exp2(-target_power * power), 0.0)
                    scaled = values * scale_v
                    for k in range(tile // 8):
                        sums[pair] = sums[pair] + scaled[k * 8 : (k + 1) * 8]
                    high, low = split2(scaled)
                    k1[pair, rows, :] = high
                    k2[pair, rows, :] = low
            for pair in pairs:
                row_totals[pair] = jnp.sum(sums[pair], axis=0, keepdims=True)

        def moved(pair):
            mass = numbers[pair] * scale_u[pair] * row_totals[pair]
            return jnp.where(valid[pair], mass, 0.0)

        def advance(pair, fates):
            width = cells if pair > first else LANES
            share = jnp.where(valid[pair], 1.0 / row_totals[pair], 0.0)
            f1, f2 = split2(fates)
            high, low = k1[pair, :, :width], k2[pair, :, :width]
            if pair == n_pair - 1:
                sums = dot(f1, high, ((1,), (0,)))
            else:
                sums = dot(jnp.concatenate([f1, f2], axis=0), high, ((1,), (0,)))
                sums = sums[:CLASSES] + sums[CLASSES:]
            sums = sums + dot(f1, low, ((1,), (0,)))
            return sums * share[:, :width]

        lead = range(stop - 1, first if odd else first - 1, -1)
        arrive(0)
        prepare(0)
        for pair in lead:
            fill(pair, 0, 0)
        arrive(1)
        prepare(1)
        for pair in lead:
            fill(pair, 0, 1)
            fill(pair, 1, 0)
            fill(pair, 1, 1)
        settle(lead)
        if odd:
            classes = lax.broadcasted_iota(jnp.int32, (CLASSES, cells), 0).astype(jnp.float32)
            fates = jnp.where((extra(n_pair) == classes) & valid[n_pair], 1.0, 0.0)
        else:
            f_copy.wait_recv()
            fates = fin[...]
        own = {}
        for pair in range(stop - 1, first, -1):
            fates = advance(pair, fates)
            own[pair] = fates[:, :LANES]
        if odd:
            fout[...] = fates
            f_copy.start()
            for pair in lead:
                results[pair, :CLASSES] = own[pair]
                results[pair, CLASSES:] = jnp.broadcast_to(moved(pair)[:, :LANES], (8, LANES))
                result_copy(pair).start()
            for part in range(2):
                for other in range(2):
                    fill(first, part, other)
            settle([first])
        fates = advance(first, fates)
        fates_ref[0] = fates[:, :tile]
        mass_ref[...] = moved(first)[:, :tile]
        number = n_block - 1
        if odd:
            number = 2 * number + 2 * n_block
            f_copy.wait_send()
            for pair in lead:
                result_copy(pair).wait_send()
        arrival(blocks(0, 0, number), x_recv.at[0, 0]).wait_send()

    for pair in range(n_pair):
        pl.when(pair_at == pair)(functools.partial(body if pair < 2 else only_send, pair))


def written(fates_ref, mass_ref, fates_out, mass_out, sems):
    copies = (
        pltpu.make_async_copy(mass_ref, mass_out, sems.at[0]),
        pltpu.make_async_copy(fates_ref, fates_out, sems.at[1]),
    )
    for copy in copies:
        copy.start()
    for copy in copies:
        copy.wait()


def per_device_fused(coords, final_coords, growth, counts, labels):
    pca, tile = coords.shape[1], coords.shape[2]
    n_pair = lax.axis_size("pair")
    n_row = lax.axis_size("row")
    n_col = lax.axis_size("col")
    n_block = n_row * n_col
    cells = n_block * tile
    vmem = pl.BlockSpec(memory_space=pltpu.VMEM)
    dma = pltpu.SemaphoreType.DMA
    fates, mass = pl.pallas_call(
        functools.partial(fused, (n_pair, n_row, n_col, tile)),
        out_shape=(
            pltpu.VMEM((1, CLASSES, tile), jnp.float32),
            pltpu.VMEM((1, tile), jnp.float32),
        ),
        in_specs=[pl.BlockSpec(memory_space=pl.ANY)] * 5,
        out_specs=(vmem, vmem),
        scratch_shapes=[
            pltpu.SMEM((n_pair + 1,), jnp.int32),
            pltpu.VMEM((pca, 1, tile), jnp.float32),
            pltpu.VMEM((pca, tile), jnp.float32),
            pltpu.VMEM((1, tile), jnp.float32),
            pltpu.VMEM((1, tile), jnp.int32),
            pltpu.VMEM(((n_pair + 1) * n_block, HALF, LANES), jnp.float32),
            pltpu.VMEM((n_pair, cells, cells), jnp.float32),
            pltpu.VMEM((n_pair, cells, cells), jnp.bfloat16),
            pltpu.VMEM((n_pair, cells, cells), jnp.bfloat16),
            pltpu.VMEM((CLASSES, cells), jnp.float32),
            pltpu.VMEM((CLASSES, cells), jnp.float32),
            pltpu.VMEM((n_pair, CLASSES + 8, LANES), jnp.float32),
            dma((5,)),
            dma,
            dma((n_pair + 1, 2)),
            dma,
            dma,
            pltpu.SemaphoreType.REGULAR,
        ],
        compiler_params=pltpu.CompilerParams(collective_id=0, has_side_effects=True),
    )(counts, jnp.transpose(coords, (1, 0, 2)), final_coords, growth, labels[None, :])
    return pl.pallas_call(
        written,
        out_shape=(
            jax.ShapeDtypeStruct(fates.shape, jnp.float32),
            jax.ShapeDtypeStruct(mass.shape, jnp.float32),
        ),
        in_specs=(vmem, vmem),
        out_specs=(pl.BlockSpec(memory_space=pl.ANY), pl.BlockSpec(memory_space=pl.ANY)),
        scratch_shapes=[dma((2,))],
    )(*(pltpu.with_memory_space_constraint(array, pltpu.VMEM) for array in (fates, mass)))


def solution(mesh):
    placed = (
        P("pair", None, ("row", "col")),
        P(None, ("row", "col")),
        P("pair", ("row", "col")),
        P(),
        P(("row", "col")),
    )
    out = (P("pair", None, ("row", "col")), P("pair", ("row", "col")))

    def whole(coords, final_coords, growth, counts, labels):
        cells = coords.shape[2]
        pairs = mesh.shape["pair"]
        blocks = mesh.shape["row"] * mesh.shape["col"]
        fits = (
            2 * cells == LANES * blocks
            and mesh.shape["row"] % 2 == 0
            and mesh.shape["col"] > 1
            and pairs > 2
            and coords.shape[0] == pairs
            and coords.shape[1] + 2 <= PIECES
            and 8 * pairs * cells * cells <= FUSED_BYTES
        )
        body = per_device_fused if fits else per_device
        return jax.shard_map(
            body, mesh=mesh, in_specs=placed, out_specs=out, check_vma=False
        )(coords, final_coords, growth, counts, labels)

    return whole
```

```python
import functools
import jax
import jax.numpy as jnp
from jax import lax
from jax.experimental import pallas as pl
from jax.experimental.pallas import tpu as pltpu
from jax.sharding import PartitionSpec as P

CLASSES = 16
FUSED_BYTES = 16 * 1024 * 1024


cost_scale = 1.0
source_power = 0.5
target_power = 50.0 / 51.0


def shifted_2(block, axis, distance):
    devices = range(lax.axis_size(axis))
    route = [(i - distance, i) for i in devices if i - distance in devices]
    return lax.ppermute(block, axis, route)


def kernel_tile(sources, targets):
    cross = lax.dot_general(
        sources,
        targets,
        (((0,), (0,)), ((), ())),
        precision=lax.Precision.HIGHEST,
        preferred_element_type=jnp.float32,
    )
    source_norms = jnp.sum(sources * sources, axis=0)
    target_norms = jnp.sum(targets * targets, axis=0)
    return jnp.exp(-(source_norms[:, None] + target_norms[None, :] - 2.0 * cross) / cost_scale)


def forward(kernel, weights):
    return lax.dot_general(
        weights,
        kernel,
        (((1,), (1,)), ((), ())),
        precision=lax.Precision.HIGHEST,
        preferred_element_type=jnp.float32,
    )


def backward(kernel, scales):
    return jnp.dot(
        scales, kernel, precision=lax.Precision.HIGHEST, preferred_element_type=jnp.float32
    )


def per_device(coords, final_coords, growth, counts, labels):
    tile = coords.shape[2]
    n_pair = lax.axis_size("pair")
    n_row = lax.axis_size("row")
    n_col = lax.axis_size("col")
    pair_at = lax.axis_index("pair")
    row_at = lax.axis_index("row")
    col_at = lax.axis_index("col")
    source_count = n_col * tile
    target_count = n_row * tile
    own_coords = coords[0]
    sources, source_growth = (
        lax.all_gather(own_coords, "col", axis=1, tiled=True),
        lax.all_gather(growth[0], "col", axis=0, tiled=True),
    )
    shifted = shifted_2(own_coords, "pair", -1)
    is_last = pair_at == n_pair - 1
    own_targets = jnp.where(is_last, final_coords, shifted)
    label_values = labels.astype(jnp.float32)
    position = lax.iota(jnp.int32, target_count)
    targets, target_labels = (
        lax.all_gather(own_targets, "row", axis=1, tiled=True),
        lax.all_gather(label_values, "row", axis=0, tiled=True),
    )
    target_index = position // tile * (n_col * tile) + col_at * tile + position % tile

    def hand_over(fates_now):
        incoming = shifted_2(fates_now, "pair", -1)
        return lax.all_gather(incoming, "row", axis=1, tiled=True)

    source_number = counts[pair_at]
    target_number = counts[pair_at + 1]
    source_total = source_number.astype(jnp.float32)
    target_total = target_number.astype(jnp.float32)
    source_index = row_at * source_count + lax.iota(jnp.int32, source_count)
    source_valid = source_index < source_number
    target_valid = target_index < target_number
    kernel = kernel_tile(sources, targets)
    start_terms = forward(kernel, target_valid.astype(jnp.float32)[None, :])[0]
    start_rows = lax.psum(start_terms, "col")
    source_mass = jnp.where(source_valid, source_growth / source_total, 0.0)
    scale_u = jnp.where(source_valid, jnp.power(source_mass / start_rows, source_power), 0.0)
    column_terms = backward(kernel, scale_u)
    column_totals = lax.psum(column_terms, "row")
    target_mass = target_valid.astype(jnp.float32) / target_total
    scale_v = jnp.where(target_valid, jnp.power(target_mass / column_totals, target_power), 0.0)
    own_offset = col_at * tile
    own_valid = lax.dynamic_slice_in_dim(source_valid, own_offset, tile, 0)
    own_scale = lax.dynamic_slice_in_dim(scale_u, own_offset, tile, 0)
    class_values = lax.iota(jnp.int32, CLASSES).astype(jnp.float32)
    label_table = jnp.where(
        (target_labels[None, :] == class_values[:, None]) & target_valid[None, :], 1.0, 0.0
    ).astype(jnp.float32)
    empty = jnp.zeros((CLASSES, tile), jnp.float32)
    final_terms = forward(kernel, scale_v[None, :])[0]
    final_rows = lax.psum(final_terms, "col")
    own_rows = lax.dynamic_slice_in_dim(final_rows, own_offset, tile, 0)
    safe_rows = jnp.where(own_valid, own_rows, 1.0)

    def advance(turn, fates_now):
        carried = jnp.where(is_last, label_table, hand_over(fates_now))
        terms = forward(kernel, carried * scale_v[None, :])
        sums = lax.psum_scatter(terms, "col", scatter_dimension=1, tiled=True)
        return jnp.where(own_valid[None, :], sums / safe_rows[None, :], 0.0)

    fates = lax.fori_loop(0, n_pair, advance, empty)
    mass = jnp.where(own_valid, source_total * own_scale * own_rows, 0.0)
    return (fates[None], mass[None])


LANES = 128
PIECES = 32
HALF = 16
BIG = 1e30
LOG2E = 1.4426950408889634
MESH = pl.DeviceIdType.MESH


def split3(a):
    first = a.astype(jnp.bfloat16)
    rest = a - first.astype(jnp.float32)
    second = rest.astype(jnp.bfloat16)
    third = (rest - second.astype(jnp.float32)).astype(jnp.bfloat16)
    return first, second, third


def split2(a):
    first = a.astype(jnp.bfloat16)
    return first, (a - first.astype(jnp.float32)).astype(jnp.bfloat16)


def dot(a, b, dims):
    return lax.dot_general(a, b, (dims, ((), ())), preferred_element_type=jnp.float32)


def packed(block, extra):
    low = block[:HALF]
    rest = block.shape[0] - HALF
    fill = jnp.zeros((HALF - rest - 1, block.shape[1]), jnp.float32)
    high = jnp.concatenate([block[HALF:], extra, fill], axis=0)
    return jnp.concatenate([low, high], axis=1)


def unpacked(ref, start, stop):
    lows, highs = [], []
    lane = lax.broadcasted_iota(jnp.int32, (HALF, LANES), 1)
    for slot in range(start, stop, 2):
        a, b = ref[slot], ref[slot + 1]
        swap_a, swap_b = pltpu.roll(a, LANES // 2, 1), pltpu.roll(b, LANES // 2, 1)
        lows.append(jnp.where(lane < LANES // 2, a, swap_b))
        highs.append(jnp.where(lane < LANES // 2, swap_a, b))
    low, high = jnp.concatenate(lows, axis=1), jnp.concatenate(highs, axis=1)
    return jnp.concatenate([low, high], axis=0)


def fused(
    sizes,
    counts_in,
    coords_in,
    final_in,
    growth_in,
    labels_in,
    fates_ref,
    mass_ref,
    counts_ref,
    coords_ref,
    final_ref,
    growth_ref,
    labels_ref,
    xg,
    kernel,
    k1,
    k2,
    fin,
    fout,
    results,
    own_sems,
    x_send,
    x_recv,
    f_recv,
    result_recv,
    ready,
):
    n_pair, n_row, n_col, tile = sizes
    n_block = n_row * n_col
    near = n_block - n_row
    cells = n_block * tile
    pca = coords_in.shape[0]
    pair_at = lax.axis_index("pair")
    row_at = lax.axis_index("row")
    col_at = lax.axis_index("col")

    def place(slot):
        along, down = divmod(slot, n_row)
        return (row_at + down) % n_row, (col_at + along) % n_col

    barrier = pltpu.get_barrier_semaphore()
    mine = col_at * n_row + row_at

    def at(block):
        return block % n_row, block // n_row

    def signal(semaphore, pair, block):
        pl.semaphore_signal(
            semaphore, inc=1, device_id=(pair, *at(block)), device_id_type=MESH
        )

    def loop(start, stop, act):
        def step(block, carry):
            act(block)
            return carry

        lax.fori_loop(start, stop, step, 0)

    count_load = pltpu.make_async_copy(counts_in, counts_ref, own_sems.at[4])
    own_loads = (
        pltpu.make_async_copy(coords_in, coords_ref, own_sems.at[0]),
        pltpu.make_async_copy(growth_in, growth_ref, own_sems.at[1]),
        pltpu.make_async_copy(final_in, final_ref, own_sems.at[2]),
        pltpu.make_async_copy(labels_in, labels_ref, own_sems.at[3]),
    )
    def block_copy(time, pair, block):
        row, col = at(block)
        there = (col_at - col) % n_col * n_row + (row_at - row) % n_row
        return pltpu.make_async_remote_copy(
            src_ref=xg.at[time * n_block],
            dst_ref=xg.at[time * n_block + there],
            send_sem=x_send,
            recv_sem=x_recv.at[time, there // near],
            device_id=(pair, row, col),
            device_id_type=MESH,
        )

    parts = ((0, near), (near, n_block))
    below = jnp.maximum(pair_at - 1, 0)

    def blocks(time, start, number):
        return xg.at[pl.ds(time * n_block + start, number)]

    def relay(time, part):
        start, stop = parts[part]
        block = blocks(time, start, stop - start)
        return pltpu.make_async_remote_copy(
            src_ref=block,
            dst_ref=block,
            send_sem=x_send,
            recv_sem=x_recv.at[time, part],
            device_id=(below, row_at, col_at),
            device_id_type=MESH,
        )

    f_copy = pltpu.make_async_remote_copy(
        src_ref=fout,
        dst_ref=fin,
        send_sem=x_send,
        recv_sem=f_recv,
        device_id=(below, row_at, col_at),
        device_id_type=MESH,
    )

    def arrival(buffer, sem):
        return pltpu.make_async_remote_copy(
            src_ref=buffer,
            dst_ref=buffer,
            send_sem=x_send,
            recv_sem=sem,
            device_id=(pair_at, row_at, col_at),
            device_id_type=MESH,
        )

    def inner(block):
        row, col = at(block)
        return (row > 0 and col > 0, -row - col, row)

    order = sorted(range(1, n_block), key=inner)

    def send(own, block):
        block_copy(own, min(own, 1), block).start()
        if own == 1:
            block_copy(n_pair, 1, block).start()

    def result_copy(pair):
        return pltpu.make_async_remote_copy(
            src_ref=results.at[pair],
            dst_ref=results.at[pair],
            send_sem=x_send,
            recv_sem=result_recv,
            device_id=(pair, row_at, col_at),
            device_id_type=MESH,
        )

    def only_send(first):
        for load in own_loads[:2]:
            load.start()
        for load in own_loads[:2]:
            load.wait()
        xg[first * n_block] = packed(coords_ref[:, 0, :], growth_ref[...])
        pl.semaphore_wait(barrier, 1)
        send(first, 0)
        pl.semaphore_wait(barrier, n_block - 1)
        for block in order:
            send(first, block)
        arrival(results.at[first], result_recv).wait_recv()
        fates_ref[0] = results[first, :CLASSES, :tile]
        mass_ref[...] = results[first, CLASSES : CLASSES + 1, :tile]
        arrival(blocks(0, 0, n_block), x_recv.at[0, 0]).wait_send()

    def body(first):
        odd = first == 1
        stop = n_pair if odd else 2
        loads = (*own_loads[: 4 if odd else 2], count_load)
        for load in loads:
            load.start()
        def allow():
            for block in (*order, 0):
                for pair in range(2, n_pair):
                    signal(barrier, pair, block)

        if odd:
            pl.when(mine == 0)(allow)
        else:
            signal(barrier, 1, mine)
        loop(mine + 1, n_block, functools.partial(signal, barrier, first))
        if odd:
            pl.semaphore_wait(barrier, mine + 1)
            pl.when(mine > 0)(allow)
        else:
            pl.when(mine > 0)(lambda: pl.semaphore_wait(barrier, mine))
        loop(0, mine, functools.partial(signal, ready, first))
        for load in loads[:-1]:
            load.wait()
        xg[first * n_block] = packed(coords_ref[:, 0, :], growth_ref[...])
        if odd:
            xg[n_pair * n_block] = packed(final_ref[...], labels_ref[...].astype(jnp.float32))
        pl.when(mine > 0)(lambda: send(first, 0))
        over = n_block - 1 - mine
        pl.when(over > 0)(lambda: pl.semaphore_wait(ready, over))
        for block in order:
            pl.when(mine != block)(functools.partial(send, first, block))
        count_load.wait()
        lane = lax.broadcasted_iota(jnp.int32, (1, LANES), 1)
        pieces = []
        for slot in range(0, n_block, 2):
            bases = []
            for one in (slot, slot + 1):
                row, col = place(one)
                bases.append((row * n_col + col) * tile)
            pieces.append(jnp.where(lane < tile, bases[0] + lane, bases[1] + lane - tile))
        index = jnp.concatenate(pieces, axis=1)
        valid = {time: index < counts_ref[time] for time in range(first, stop + 1)}
        numbers = {time: counts_ref[time].astype(jnp.float32) for time in range(first, stop + 1)}
        lefts, rights, extras, totals = {}, {}, {}, {}

        def arrive(part):
            for time in range(first, stop + 1):
                start, end = parts[part]
                if part == 0 and (time == first or (odd and time == n_pair)):
                    start = 1
                arrival(blocks(time, start, end - start), x_recv.at[time, part]).wait_recv()
                if odd and time < first + 2:
                    relay(time, part).start()

        def prepare(part):
            start, end = parts[part]
            width = (end - start) * tile
            lanes = slice(start * tile, end * tile)
            feature = lax.broadcasted_iota(jnp.int32, (PIECES, width), 0)
            for time in range(first, stop + 1):
                z = unpacked(xg, time * n_block + start, time * n_block + end)
                extras[time, part] = z[pca : pca + 1]
                z = jnp.where(feature < pca, z, 0.0)
                norm = jnp.sum(z * z, axis=0, keepdims=True) * LOG2E
                if time < stop:
                    a = jnp.where(
                        feature < pca, z * (2.0 * LOG2E), jnp.where(feature == pca, -norm, 1.0)
                    )
                    a1, a2, a3 = split3(a)
                    rights[time, part] = jnp.concatenate([a1, a2, a1, a2, a3, a1], axis=0)
                if time > first:
                    low = jnp.where(valid[time][:, lanes], -norm, -BIG)
                    b = jnp.where(feature < pca, z, jnp.where(feature == pca, 1.0, low))
                    b1, b2, b3 = split3(b)
                    lefts[time, part] = jnp.concatenate([b1, b1, b2, b2, b1, b3], axis=0)

        def fill(pair, part, other):
            first_row, first_lane = parts[part][0] * tile, parts[other][0] * tile
            left, right = lefts[pair + 1, part], rights[pair, other]
            lanes = slice(first_lane, first_lane + right.shape[1])
            total = totals.get((pair, other), jnp.zeros((8, right.shape[1]), jnp.float32))
            for j in range(left.shape[1] // LANES):
                values = jnp.exp2(dot(left[:, j * LANES : (j + 1) * LANES], right, ((0,), (0,))))
                for k in range(LANES // 8):
                    total = total + values[k * 8 : (k + 1) * 8]
                rows = slice(first_row + j * LANES, first_row + (j + 1) * LANES)
                kernel[pair, rows, lanes] = values
            totals[pair, other] = total

        def extra(time):
            return jnp.concatenate([extras[time, 0], extras[time, 1]], axis=1)

        scale_u, row_totals = {}, {}
        iota_rows = lax.broadcasted_iota(jnp.int32, (tile, 1), 0)

        def settle(pairs):
            for pair in pairs:
                total = jnp.concatenate([totals[pair, 0], totals[pair, 1]], axis=1)
                total = jnp.sum(total, axis=0, keepdims=True)
                share = jnp.sqrt(extra(pair) / numbers[pair])
                scale_u[pair] = jnp.where(valid[pair], share * lax.rsqrt(total), 0.0)
            sums = {pair: jnp.zeros((8, cells), jnp.float32) for pair in pairs}
            for slot in range(n_block):
                rows = slice(slot * tile, (slot + 1) * tile)
                row, col = place(slot)
                position = (row * n_col + col) * tile + iota_rows
                for pair in pairs:
                    values = kernel[pair, rows, :]
                    terms = values * scale_u[pair]
                    folded = terms[:, :LANES]
                    for j in range(1, cells // LANES):
                        folded = folded + terms[:, j * LANES : (j + 1) * LANES]
                    column = jnp.sum(folded, axis=1, keepdims=True)
                    is_target = position < counts_ref[pair + 1]
                    column = jnp.where(is_target, column, 1.0)
                    power = jnp.log2(column) + jnp.log2(jnp.full((tile, 1), numbers[pair + 1]))
                    scale_v = jnp.where(is_target, jnp.exp2(-target_power * power), 0.0)
                    scaled = values * scale_v
                    for k in range(tile // 8):
                        sums[pair] = sums[pair] + scaled[k * 8 : (k + 1) * 8]
                    high, low = split2(scaled)
                    k1[pair, rows, :] = high
                    k2[pair, rows, :] = low
            for pair in pairs:
                row_totals[pair] = jnp.sum(sums[pair], axis=0, keepdims=True)

        def moved(pair):
            mass = numbers[pair] * scale_u[pair] * row_totals[pair]
            return jnp.where(valid[pair], mass, 0.0)

        def advance(pair, fates):
            width = cells if pair > first else LANES
            share = jnp.where(valid[pair], 1.0 / row_totals[pair], 0.0)
            f1, f2 = split2(fates)
            high, low = k1[pair, :, :width], k2[pair, :, :width]
            if pair == n_pair - 1:
                sums = dot(f1, high, ((1,), (0,)))
            else:
                sums = dot(jnp.concatenate([f1, f2], axis=0), high, ((1,), (0,)))
                sums = sums[:CLASSES] + sums[CLASSES:]
            sums = sums + dot(f1, low, ((1,), (0,)))
            return sums * share[:, :width]

        lead = range(stop - 1, first if odd else first - 1, -1)
        arrive(0)
        prepare(0)
        for pair in lead:
            fill(pair, 0, 0)
        arrive(1)
        prepare(1)
        for pair in lead:
            fill(pair, 0, 1)
            fill(pair, 1, 0)
            fill(pair, 1, 1)
        settle(lead)
        if odd:
            classes = lax.broadcasted_iota(jnp.int32, (CLASSES, cells), 0).astype(jnp.float32)
            fates = jnp.where((extra(n_pair) == classes) & valid[n_pair], 1.0, 0.0)
        else:
            f_copy.wait_recv()
            fates = fin[...]
        own = {}
        for pair in range(stop - 1, first, -1):
            fates = advance(pair, fates)
            own[pair] = fates[:, :LANES]
        if odd:
            fout[...] = fates
            f_copy.start()
            for pair in lead:
                results[pair, :CLASSES] = own[pair]
                results[pair, CLASSES:] = jnp.broadcast_to(moved(pair)[:, :LANES], (8, LANES))
                result_copy(pair).start()
            for part in range(2):
                for other in range(2):
                    fill(first, part, other)
            settle([first])
        fates = advance(first, fates)
        fates_ref[0] = fates[:, :tile]
        mass_ref[...] = moved(first)[:, :tile]
        number = n_block - 1
        if odd:
            number = 2 * number + 2 * n_block
            f_copy.wait_send()
            for pair in lead:
                result_copy(pair).wait_send()
        arrival(blocks(0, 0, number), x_recv.at[0, 0]).wait_send()

    for pair in range(n_pair):
        pl.when(pair_at == pair)(functools.partial(body if pair < 2 else only_send, pair))


def written(fates_ref, mass_ref, fates_out, mass_out, sems):
    copies = (
        pltpu.make_async_copy(mass_ref, mass_out, sems.at[0]),
        pltpu.make_async_copy(fates_ref, fates_out, sems.at[1]),
    )
    for copy in copies:
        copy.start()
    for copy in copies:
        copy.wait()


def per_device_fused(coords, final_coords, growth, counts, labels):
    pca, tile = coords.shape[1], coords.shape[2]
    n_pair = lax.axis_size("pair")
    n_row = lax.axis_size("row")
    n_col = lax.axis_size("col")
    n_block = n_row * n_col
    cells = n_block * tile
    vmem = pl.BlockSpec(memory_space=pltpu.VMEM)
    dma = pltpu.SemaphoreType.DMA
    fates, mass = pl.pallas_call(
        functools.partial(fused, (n_pair, n_row, n_col, tile)),
        out_shape=(
            pltpu.VMEM((1, CLASSES, tile), jnp.float32),
            pltpu.VMEM((1, tile), jnp.float32),
        ),
        in_specs=[pl.BlockSpec(memory_space=pl.ANY)] * 5,
        out_specs=(vmem, vmem),
        scratch_shapes=[
            pltpu.SMEM((n_pair + 1,), jnp.int32),
            pltpu.VMEM((pca, 1, tile), jnp.float32),
            pltpu.VMEM((pca, tile), jnp.float32),
            pltpu.VMEM((1, tile), jnp.float32),
            pltpu.VMEM((1, tile), jnp.int32),
            pltpu.VMEM(((n_pair + 1) * n_block, HALF, LANES), jnp.float32),
            pltpu.VMEM((n_pair, cells, cells), jnp.float32),
            pltpu.VMEM((n_pair, cells, cells), jnp.bfloat16),
            pltpu.VMEM((n_pair, cells, cells), jnp.bfloat16),
            pltpu.VMEM((CLASSES, cells), jnp.float32),
            pltpu.VMEM((CLASSES, cells), jnp.float32),
            pltpu.VMEM((n_pair, CLASSES + 8, LANES), jnp.float32),
            dma((5,)),
            dma,
            dma((n_pair + 1, 2)),
            dma,
            dma,
            pltpu.SemaphoreType.REGULAR,
        ],
        compiler_params=pltpu.CompilerParams(collective_id=0, has_side_effects=True),
    )(counts, jnp.transpose(coords, (1, 0, 2)), final_coords, growth, labels[None, :])
    return pl.pallas_call(
        written,
        out_shape=(
            jax.ShapeDtypeStruct(fates.shape, jnp.float32),
            jax.ShapeDtypeStruct(mass.shape, jnp.float32),
        ),
        in_specs=(vmem, vmem),
        out_specs=(pl.BlockSpec(memory_space=pl.ANY), pl.BlockSpec(memory_space=pl.ANY)),
        scratch_shapes=[dma((2,))],
    )(*(pltpu.with_memory_space_constraint(array, pltpu.VMEM) for array in (fates, mass)))


def solution(mesh):
    placed = (
        P("pair", None, ("row", "col")),
        P(None, ("row", "col")),
        P("pair", ("row", "col")),
        P(),
        P(("row", "col")),
    )
    out = (P("pair", None, ("row", "col")), P("pair", ("row", "col")))

    def whole(coords, final_coords, growth, counts, labels):
        cells = coords.shape[2]
        pairs = mesh.shape["pair"]
        blocks = mesh.shape["row"] * mesh.shape["col"]
        fits = (
            2 * cells == LANES * blocks
            and mesh.shape["row"] % 2 == 0
            and mesh.shape["col"] > 1
            and pairs > 2
            and coords.shape[0] == pairs
            and coords.shape[1] + 2 <= PIECES
            and 8 * pairs * cells * cells <= FUSED_BYTES
        )
        body = per_device_fused if fits else per_device
        return jax.shard_map(
            body, mesh=mesh, in_specs=placed, out_specs=out, check_vma=False
        )(coords, final_coords, growth, counts, labels)

    return whole
```

```python
import functools
import jax
import jax.numpy as jnp
from jax import lax
from jax.experimental import pallas as pl
from jax.experimental.pallas import tpu as pltpu
from jax.sharding import PartitionSpec as P

CLASSES = 16
FUSED_BYTES = 16 * 1024 * 1024


cost_scale = 1.0
source_power = 0.5
target_power = 50.0 / 51.0


def shifted_2(block, axis, distance):
    devices = range(lax.axis_size(axis))
    route = [(i - distance, i) for i in devices if i - distance in devices]
    return lax.ppermute(block, axis, route)


def kernel_tile(sources, targets):
    cross = lax.dot_general(
        sources,
        targets,
        (((0,), (0,)), ((), ())),
        precision=lax.Precision.HIGHEST,
        preferred_element_type=jnp.float32,
    )
    source_norms = jnp.sum(sources * sources, axis=0)
    target_norms = jnp.sum(targets * targets, axis=0)
    return jnp.exp(-(source_norms[:, None] + target_norms[None, :] - 2.0 * cross) / cost_scale)


def forward(kernel, weights):
    return lax.dot_general(
        weights,
        kernel,
        (((1,), (1,)), ((), ())),
        precision=lax.Precision.HIGHEST,
        preferred_element_type=jnp.float32,
    )


def backward(kernel, scales):
    return jnp.dot(
        scales, kernel, precision=lax.Precision.HIGHEST, preferred_element_type=jnp.float32
    )


def per_device(coords, final_coords, growth, counts, labels):
    tile = coords.shape[2]
    n_pair = lax.axis_size("pair")
    n_row = lax.axis_size("row")
    n_col = lax.axis_size("col")
    pair_at = lax.axis_index("pair")
    row_at = lax.axis_index("row")
    col_at = lax.axis_index("col")
    source_count = n_col * tile
    target_count = n_row * tile
    own_coords = coords[0]
    sources, source_growth = (
        lax.all_gather(own_coords, "col", axis=1, tiled=True),
        lax.all_gather(growth[0], "col", axis=0, tiled=True),
    )
    shifted = shifted_2(own_coords, "pair", -1)
    is_last = pair_at == n_pair - 1
    own_targets = jnp.where(is_last, final_coords, shifted)
    label_values = labels.astype(jnp.float32)
    position = lax.iota(jnp.int32, target_count)
    targets, target_labels = (
        lax.all_gather(own_targets, "row", axis=1, tiled=True),
        lax.all_gather(label_values, "row", axis=0, tiled=True),
    )
    target_index = position // tile * (n_col * tile) + col_at * tile + position % tile

    def hand_over(fates_now):
        incoming = shifted_2(fates_now, "pair", -1)
        return lax.all_gather(incoming, "row", axis=1, tiled=True)

    source_number = counts[pair_at]
    target_number = counts[pair_at + 1]
    source_total = source_number.astype(jnp.float32)
    target_total = target_number.astype(jnp.float32)
    source_index = row_at * source_count + lax.iota(jnp.int32, source_count)
    source_valid = source_index < source_number
    target_valid = target_index < target_number
    kernel = kernel_tile(sources, targets)
    start_terms = forward(kernel, target_valid.astype(jnp.float32)[None, :])[0]
    start_rows = lax.psum(start_terms, "col")
    source_mass = jnp.where(source_valid, source_growth / source_total, 0.0)
    scale_u = jnp.where(source_valid, jnp.power(source_mass / start_rows, source_power), 0.0)
    column_terms = backward(kernel, scale_u)
    column_totals = lax.psum(column_terms, "row")
    target_mass = target_valid.astype(jnp.float32) / target_total
    scale_v = jnp.where(target_valid, jnp.power(target_mass / column_totals, target_power), 0.0)
    own_offset = col_at * tile
    own_valid = lax.dynamic_slice_in_dim(source_valid, own_offset, tile, 0)
    own_scale = lax.dynamic_slice_in_dim(scale_u, own_offset, tile, 0)
    class_values = lax.iota(jnp.int32, CLASSES).astype(jnp.float32)
    label_table = jnp.where(
        (target_labels[None, :] == class_values[:, None]) & target_valid[None, :], 1.0, 0.0
    ).astype(jnp.float32)
    empty = jnp.zeros((CLASSES, tile), jnp.float32)
    final_terms = forward(kernel, scale_v[None, :])[0]
    final_rows = lax.psum(final_terms, "col")
    own_rows = lax.dynamic_slice_in_dim(final_rows, own_offset, tile, 0)
    safe_rows = jnp.where(own_valid, own_rows, 1.0)

    def advance(turn, fates_now):
        carried = jnp.where(is_last, label_table, hand_over(fates_now))
        terms = forward(kernel, carried * scale_v[None, :])
        sums = lax.psum_scatter(terms, "col", scatter_dimension=1, tiled=True)
        return jnp.where(own_valid[None, :], sums / safe_rows[None, :], 0.0)

    fates = lax.fori_loop(0, n_pair, advance, empty)
    mass = jnp.where(own_valid, source_total * own_scale * own_rows, 0.0)
    return (fates[None], mass[None])


LANES = 128
PIECES = 32
HALF = 16
BIG = 1e30
SCALE = 1.6986436005760381
MESH = pl.DeviceIdType.MESH


def split3(a):
    first = a.astype(jnp.bfloat16)
    rest = a - first.astype(jnp.float32)
    second = rest.astype(jnp.bfloat16)
    third = (rest - second.astype(jnp.float32)).astype(jnp.bfloat16)
    return first, second, third


def split2(a):
    first = a.astype(jnp.bfloat16)
    return first, (a - first.astype(jnp.float32)).astype(jnp.bfloat16)


def dot(a, b, dims):
    return lax.dot_general(a, b, (dims, ((), ())), preferred_element_type=jnp.float32)


def packed(block, extra):
    low = block[:HALF]
    rest = block.shape[0] - HALF
    fill = jnp.zeros((HALF - rest - 1, block.shape[1]), jnp.float32)
    high = jnp.concatenate([block[HALF:], extra, fill], axis=0)
    return jnp.concatenate([low, high], axis=1)


def unpacked(ref, start, stop):
    lows, highs = [], []
    lane = lax.broadcasted_iota(jnp.int32, (HALF, LANES), 1)
    for slot in range(start, stop, 2):
        a, b = ref[slot], ref[slot + 1]
        swap_a, swap_b = pltpu.roll(a, LANES // 2, 1), pltpu.roll(b, LANES // 2, 1)
        lows.append(jnp.where(lane < LANES // 2, a, swap_b))
        highs.append(jnp.where(lane < LANES // 2, swap_a, b))
    low, high = jnp.concatenate(lows, axis=1), jnp.concatenate(highs, axis=1)
    return jnp.concatenate([low, high], axis=0)


def fused(
    sizes,
    counts_in,
    coords_in,
    final_in,
    growth_in,
    labels_in,
    fates_ref,
    mass_ref,
    counts_ref,
    coords_ref,
    final_ref,
    growth_ref,
    labels_ref,
    xg,
    kernel,
    k1,
    k2,
    fin,
    fout,
    results,
    own_sems,
    x_send,
    x_recv,
    f_recv,
    result_recv,
    ready,
):
    n_pair, n_row, n_col, tile = sizes
    n_block = n_row * n_col
    near = n_block - n_row
    cells = n_block * tile
    pca = coords_in.shape[0]
    pair_at = lax.axis_index("pair")
    row_at = lax.axis_index("row")
    col_at = lax.axis_index("col")

    def place(slot):
        along, down = divmod(slot, n_row)
        return (row_at + down) % n_row, (col_at + along) % n_col

    barrier = pltpu.get_barrier_semaphore()
    mine = col_at * n_row + row_at

    def at(block):
        return block % n_row, block // n_row

    def signal(semaphore, pair, block):
        pl.semaphore_signal(
            semaphore, inc=1, device_id=(pair, *at(block)), device_id_type=MESH
        )

    def loop(start, stop, act):
        def step(block, carry):
            act(block)
            return carry

        lax.fori_loop(start, stop, step, 0)

    count_load = pltpu.make_async_copy(counts_in, counts_ref, own_sems.at[2])
    own_loads = (
        pltpu.make_async_copy(coords_in, coords_ref, own_sems.at[0]),
        pltpu.make_async_copy(growth_in, growth_ref, own_sems.at[1]),
        pltpu.make_async_copy(final_in, final_ref, f_recv),
        pltpu.make_async_copy(labels_in, labels_ref, result_recv),
    )
    for load in own_loads[:2]:
        load.start()

    def block_copy(time, pair, block):
        row, col = at(block)
        there = (col_at - col) % n_col * n_row + (row_at - row) % n_row
        return pltpu.make_async_remote_copy(
            src_ref=xg.at[time * n_block],
            dst_ref=xg.at[time * n_block + there],
            send_sem=x_send,
            recv_sem=x_recv.at[time - pair, there // near],
            device_id=(pair, row, col),
            device_id_type=MESH,
        )

    parts = ((0, near), (near, n_block))
    below = jnp.maximum(pair_at - 1, 0)

    def blocks(time, start, number):
        return xg.at[pl.ds(time * n_block + start, number)]

    def relay(time, part):
        start, stop = parts[part]
        block = blocks(time, start, stop - start)
        return pltpu.make_async_remote_copy(
            src_ref=block,
            dst_ref=block,
            send_sem=x_send,
            recv_sem=x_recv.at[time, part],
            device_id=(below, row_at, col_at),
            device_id_type=MESH,
        )

    f_copy = pltpu.make_async_remote_copy(
        src_ref=fout,
        dst_ref=fin,
        send_sem=x_send,
        recv_sem=f_recv,
        device_id=(below, row_at, col_at),
        device_id_type=MESH,
    )

    def arrival(buffer, sem):
        return pltpu.make_async_remote_copy(
            src_ref=buffer,
            dst_ref=buffer,
            send_sem=x_send,
            recv_sem=sem,
            device_id=(pair_at, row_at, col_at),
            device_id_type=MESH,
        )

    def inner(block):
        row, col = at(block)
        return (row > 0 and col > 0, -row - col, row)

    order = sorted(range(1, n_block), key=inner)

    def send(own, block):
        block_copy(own, min(own, 1), block).start()
        if own == 1:
            block_copy(n_pair, 1, block).start()

    def result_copy(pair):
        return pltpu.make_async_remote_copy(
            src_ref=results.at[pair],
            dst_ref=results.at[pair],
            send_sem=x_send,
            recv_sem=result_recv,
            device_id=(pair, row_at, col_at),
            device_id_type=MESH,
        )

    def only_send(first):
        for load in own_loads[:2]:
            load.wait()
        xg[first * n_block] = packed(coords_ref[:, 0, :], growth_ref[...])
        pl.semaphore_wait(barrier, 1)
        send(first, 0)
        pl.semaphore_wait(barrier, n_block - 1)
        for block in order:
            send(first, block)
        arrival(results.at[first], result_recv).wait_recv()
        fates_ref[0] = results[first, :CLASSES, :tile]
        mass_ref[...] = results[first, CLASSES : CLASSES + 1, :tile]
        arrival(blocks(0, 0, n_block), x_recv.at[0, 0]).wait_send()

    def body(first):
        odd = first == 1
        stop = n_pair if odd else 2
        loads = (*own_loads[: 4 if odd else 2], count_load)
        for load in loads[2:]:
            load.start()
        def allow():
            for block in (*order, 0):
                for pair in range(2, n_pair):
                    signal(barrier, pair, block)

        if odd:
            pl.when(mine == 0)(allow)
        else:
            signal(barrier, 1, mine)
        loop(mine + 1, n_block, functools.partial(signal, barrier, first))
        if odd:
            pl.semaphore_wait(barrier, mine + 1)
            pl.when(mine > 0)(allow)
        else:
            pl.when(mine > 0)(lambda: pl.semaphore_wait(barrier, mine))
        loop(0, mine, functools.partial(signal, ready, first))
        for load in loads[:-1]:
            load.wait()
        xg[first * n_block] = packed(coords_ref[:, 0, :], growth_ref[...])
        if odd:
            xg[n_pair * n_block] = packed(final_ref[...], labels_ref[...].astype(jnp.float32))
        pl.when(mine > 0)(lambda: send(first, 0))
        over = n_block - 1 - mine
        pl.when(over > 0)(lambda: pl.semaphore_wait(ready, over))
        for block in order:
            pl.when(mine != block)(functools.partial(send, first, block))
        count_load.wait()
        lane = lax.broadcasted_iota(jnp.int32, (1, LANES), 1)
        pieces = []
        for slot in range(0, n_block, 2):
            bases = []
            for one in (slot, slot + 1):
                row, col = place(one)
                bases.append((row * n_col + col) * tile)
            pieces.append(jnp.where(lane < tile, bases[0] + lane, bases[1] + lane - tile))
        index = jnp.concatenate(pieces, axis=1)
        valid = {time: index < counts_ref[time] for time in range(first, stop + 1)}
        numbers = {time: counts_ref[time].astype(jnp.float32) for time in range(first, stop + 1)}
        lefts, rights, extras, totals = {}, {}, {}, {}

        def arrive(part):
            for time in range(first, stop + 1):
                start, end = parts[part]
                if part == 0 and (time == first or (odd and time == n_pair)):
                    start = 1
                arrival(blocks(time, start, end - start), x_recv.at[time - first, part]).wait_recv()
                if odd and time < first + 2:
                    relay(time, part).start()

        def prepare(part):
            start, end = parts[part]
            width = (end - start) * tile
            lanes = slice(start * tile, end * tile)
            feature = lax.broadcasted_iota(jnp.int32, (PIECES, width), 0)
            for time in range(first, stop + 1):
                z = unpacked(xg, time * n_block + start, time * n_block + end)
                extras[time, part] = z[pca : pca + 1]
                z = jnp.where(feature < pca, z * SCALE, 0.0)
                norm = jnp.sum(z * z, axis=0, keepdims=True) * 0.5
                q = jnp.where(feature < pca, z, jnp.where(feature == pca, -norm, 1.0))
                q1, q2, q3 = split3(q)
                if time < stop:
                    rights[time, part] = jnp.concatenate([q1, q2, q1, q2, q3, q1], axis=0)
                if time > first:
                    low = jnp.where(valid[time][:, lanes], -norm, -BIG)
                    ends = jnp.where(feature[HALF:] == pca, 1.0, low)
                    pieces_of = [
                        jnp.concatenate(
                            [one[:HALF], jnp.where(feature[HALF:] < pca, one[HALF:], end)], axis=0
                        )
                        for one, end in zip((q1, q2, q3), split3(ends), strict=True)
                    ]
                    b1, b2, b3 = pieces_of
                    lefts[time, part] = jnp.concatenate([b1, b1, b2, b2, b1, b3], axis=0)

        def fill(pair, part, other):
            first_row, first_lane = parts[part][0] * tile, parts[other][0] * tile
            left, right = lefts[pair + 1, part], rights[pair, other]
            lanes = slice(first_lane, first_lane + right.shape[1])
            total = totals.get((pair, other), jnp.zeros((8, right.shape[1]), jnp.float32))
            for j in range(left.shape[1] // LANES):
                values = jnp.exp2(dot(left[:, j * LANES : (j + 1) * LANES], right, ((0,), (0,))))
                for k in range(LANES // 8):
                    total = total + values[k * 8 : (k + 1) * 8]
                rows = slice(first_row + j * LANES, first_row + (j + 1) * LANES)
                kernel[pair, rows, lanes] = values
            totals[pair, other] = total

        def extra(time):
            return jnp.concatenate([extras[time, 0], extras[time, 1]], axis=1)

        scale_u, row_totals = {}, {}
        iota_rows = lax.broadcasted_iota(jnp.int32, (tile, 1), 0)

        def settle(pairs):
            for pair in pairs:
                total = jnp.concatenate([totals[pair, 0], totals[pair, 1]], axis=1)
                total = jnp.sum(total, axis=0, keepdims=True)
                share = jnp.sqrt(extra(pair) / numbers[pair])
                scale_u[pair] = jnp.where(valid[pair], share * lax.rsqrt(total), 0.0)
            sums = {pair: jnp.zeros((8, cells), jnp.float32) for pair in pairs}
            for slot in range(n_block):
                rows = slice(slot * tile, (slot + 1) * tile)
                row, col = place(slot)
                position = (row * n_col + col) * tile + iota_rows
                for pair in pairs:
                    values = kernel[pair, rows, :]
                    terms = values * scale_u[pair]
                    folded = terms[:, :LANES]
                    for j in range(1, cells // LANES):
                        folded = folded + terms[:, j * LANES : (j + 1) * LANES]
                    column = jnp.sum(folded, axis=1, keepdims=True)
                    is_target = position < counts_ref[pair + 1]
                    column = jnp.where(is_target, column, 1.0)
                    power = jnp.log2(column) + jnp.log2(jnp.full((tile, 1), numbers[pair + 1]))
                    scale_v = jnp.where(is_target, jnp.exp2(-target_power * power), 0.0)
                    scaled = values * scale_v
                    for k in range(tile // 8):
                        sums[pair] = sums[pair] + scaled[k * 8 : (k + 1) * 8]
                    high, low = split2(scaled)
                    k1[pair, rows, :] = high
                    k2[pair, rows, :] = low
            for pair in pairs:
                row_totals[pair] = jnp.sum(sums[pair], axis=0, keepdims=True)

        def moved(pair):
            mass = numbers[pair] * scale_u[pair] * row_totals[pair]
            return jnp.where(valid[pair], mass, 0.0)

        def advance(pair, fates):
            width = cells if pair > first else LANES
            share = jnp.where(valid[pair], 1.0 / row_totals[pair], 0.0)
            f1, f2 = split2(fates)
            high, low = k1[pair, :, :width], k2[pair, :, :width]
            if pair == n_pair - 1:
                sums = dot(f1, high, ((1,), (0,)))
            else:
                sums = dot(jnp.concatenate([f1, f2], axis=0), high, ((1,), (0,)))
                sums = sums[:CLASSES] + sums[CLASSES:]
            sums = sums + dot(f1, low, ((1,), (0,)))
            return sums * share[:, :width]

        lead = range(stop - 1, first if odd else first - 1, -1)
        arrive(0)
        prepare(0)
        for pair in lead:
            fill(pair, 0, 0)
        arrive(1)
        prepare(1)
        for pair in lead:
            fill(pair, 0, 1)
            fill(pair, 1, 0)
            fill(pair, 1, 1)
        settle(lead)
        share = {pair: jnp.where(valid[pair], 1.0 / row_totals[pair], 0.0) for pair in lead}
        if odd:
            classes = lax.broadcasted_iota(jnp.int32, (CLASSES, cells), 0).astype(jnp.float32)
            fates = jnp.where((extra(n_pair) == classes) & valid[n_pair], 1.0, 0.0)
        else:
            turned = jnp.transpose(jnp.broadcast_to(share[1], (8, cells)))[:, :1]
            near_high, near_low = k1[0, :, :LANES], k2[0, :, :LANES]
            scaled = (near_high.astype(jnp.float32) + near_low.astype(jnp.float32)) * turned
            b1, b2 = split2(scaled)
            both = dot(k1[1], jnp.concatenate([b1, b2], axis=1), ((1,), (0,)))
            chain = both[:, :LANES] + both[:, LANES:] + dot(k2[1], b1, ((1,), (0,)))
            h1, h2 = split2(chain)
            f_copy.wait_recv()
            f1, f2 = split2(fin[...])
            both = dot(jnp.concatenate([f1, f2], axis=0), h1, ((1,), (0,)))
            both = both[:CLASSES] + both[CLASSES:] + dot(f1, h2, ((1,), (0,)))
            fates = both * share[0][:, :LANES]
        own = {}
        for pair in lead if odd else ():
            fates = advance(pair, fates)
            own[pair] = fates[:, :LANES]
        if odd:
            fout[...] = fates
            f_copy.start()
            for pair in lead:
                results[pair, :CLASSES] = own[pair]
                results[pair, CLASSES:] = jnp.broadcast_to(moved(pair)[:, :LANES], (8, LANES))
                result_copy(pair).start()
            for part in range(2):
                for other in range(2):
                    fill(first, part, other)
            settle([first])
            fates = advance(first, fates)
        fates_ref[0] = fates[:, :tile]
        mass_ref[...] = moved(first)[:, :tile]
        number = n_block - 1
        if odd:
            number = 2 * number + 2 * n_block
            f_copy.wait_send()
            for pair in lead:
                result_copy(pair).wait_send()
        arrival(blocks(0, 0, number), x_recv.at[0, 0]).wait_send()

    for pair in range(n_pair):
        pl.when(pair_at == pair)(functools.partial(body if pair < 2 else only_send, pair))


def written(fates_ref, mass_ref, fates_out, mass_out, sems):
    copies = (
        pltpu.make_async_copy(mass_ref, mass_out, sems.at[0]),
        pltpu.make_async_copy(fates_ref, fates_out, sems.at[1]),
    )
    for copy in copies:
        copy.start()
    for copy in copies:
        copy.wait()


def per_device_fused(coords, final_coords, growth, counts, labels):
    pca, tile = coords.shape[1], coords.shape[2]
    n_pair = lax.axis_size("pair")
    n_row = lax.axis_size("row")
    n_col = lax.axis_size("col")
    n_block = n_row * n_col
    cells = n_block * tile
    vmem = pl.BlockSpec(memory_space=pltpu.VMEM)
    dma = pltpu.SemaphoreType.DMA
    fates, mass = pl.pallas_call(
        functools.partial(fused, (n_pair, n_row, n_col, tile)),
        out_shape=(
            pltpu.VMEM((1, CLASSES, tile), jnp.float32),
            pltpu.VMEM((1, tile), jnp.float32),
        ),
        in_specs=[pl.BlockSpec(memory_space=pl.ANY)] * 5,
        out_specs=(vmem, vmem),
        scratch_shapes=[
            pltpu.SMEM((n_pair + 1,), jnp.int32),
            pltpu.VMEM((pca, 1, tile), jnp.float32),
            pltpu.VMEM((pca, tile), jnp.float32),
            pltpu.VMEM((1, tile), jnp.float32),
            pltpu.VMEM((1, tile), jnp.int32),
            pltpu.VMEM(((n_pair + 1) * n_block, HALF, LANES), jnp.float32),
            pltpu.VMEM((n_pair, cells, cells), jnp.float32),
            pltpu.VMEM((n_pair, cells, cells), jnp.bfloat16),
            pltpu.VMEM((n_pair, cells, cells), jnp.bfloat16),
            pltpu.VMEM((CLASSES, cells), jnp.float32),
            pltpu.VMEM((CLASSES, cells), jnp.float32),
            pltpu.VMEM((n_pair, CLASSES + 8, LANES), jnp.float32),
            dma((3,)),
            dma,
            dma((n_pair, 2)),
            dma,
            dma,
            pltpu.SemaphoreType.REGULAR,
        ],
        compiler_params=pltpu.CompilerParams(collective_id=0, has_side_effects=True),
    )(counts, jnp.transpose(coords, (1, 0, 2)), final_coords, growth, labels[None, :])
    return pl.pallas_call(
        written,
        out_shape=(
            jax.ShapeDtypeStruct(fates.shape, jnp.float32),
            jax.ShapeDtypeStruct(mass.shape, jnp.float32),
        ),
        in_specs=(vmem, vmem),
        out_specs=(pl.BlockSpec(memory_space=pl.ANY), pl.BlockSpec(memory_space=pl.ANY)),
        scratch_shapes=[dma((2,))],
    )(*(pltpu.with_memory_space_constraint(array, pltpu.VMEM) for array in (fates, mass)))


def solution(mesh):
    placed = (
        P("pair", None, ("row", "col")),
        P(None, ("row", "col")),
        P("pair", ("row", "col")),
        P(),
        P(("row", "col")),
    )
    out = (P("pair", None, ("row", "col")), P("pair", ("row", "col")))

    def whole(coords, final_coords, growth, counts, labels):
        cells = coords.shape[2]
        pairs = mesh.shape["pair"]
        blocks = mesh.shape["row"] * mesh.shape["col"]
        fits = (
            2 * cells == LANES * blocks
            and mesh.shape["row"] % 2 == 0
            and mesh.shape["col"] > 1
            and pairs > 2
            and coords.shape[0] == pairs
            and coords.shape[1] + 2 <= PIECES
            and 8 * pairs * cells * cells <= FUSED_BYTES
        )
        body = per_device_fused if fits else per_device
        return jax.shard_map(
            body, mesh=mesh, in_specs=placed, out_specs=out, check_vma=False
        )(coords, final_coords, growth, counts, labels)

    return whole
```

```python
import functools
import jax
import jax.numpy as jnp
from jax import lax
from jax.experimental import pallas as pl
from jax.experimental.pallas import tpu as pltpu
from jax.sharding import PartitionSpec as P

CLASSES = 16
FUSED_BYTES = 16 * 1024 * 1024


cost_scale = 1.0
source_power = 0.5
target_power = 50.0 / 51.0


def shifted_2(block, axis, distance):
    devices = range(lax.axis_size(axis))
    route = [(i - distance, i) for i in devices if i - distance in devices]
    return lax.ppermute(block, axis, route)


def kernel_tile(sources, targets):
    cross = lax.dot_general(
        sources,
        targets,
        (((0,), (0,)), ((), ())),
        precision=lax.Precision.HIGHEST,
        preferred_element_type=jnp.float32,
    )
    source_norms = jnp.sum(sources * sources, axis=0)
    target_norms = jnp.sum(targets * targets, axis=0)
    return jnp.exp(-(source_norms[:, None] + target_norms[None, :] - 2.0 * cross) / cost_scale)


def forward(kernel, weights):
    return lax.dot_general(
        weights,
        kernel,
        (((1,), (1,)), ((), ())),
        precision=lax.Precision.HIGHEST,
        preferred_element_type=jnp.float32,
    )


def backward(kernel, scales):
    return jnp.dot(
        scales, kernel, precision=lax.Precision.HIGHEST, preferred_element_type=jnp.float32
    )


def per_device(coords, final_coords, growth, counts, labels):
    tile = coords.shape[2]
    n_pair = lax.axis_size("pair")
    n_row = lax.axis_size("row")
    n_col = lax.axis_size("col")
    pair_at = lax.axis_index("pair")
    row_at = lax.axis_index("row")
    col_at = lax.axis_index("col")
    source_count = n_col * tile
    target_count = n_row * tile
    own_coords = coords[0]
    sources, source_growth = (
        lax.all_gather(own_coords, "col", axis=1, tiled=True),
        lax.all_gather(growth[0], "col", axis=0, tiled=True),
    )
    shifted = shifted_2(own_coords, "pair", -1)
    is_last = pair_at == n_pair - 1
    own_targets = jnp.where(is_last, final_coords, shifted)
    label_values = labels.astype(jnp.float32)
    position = lax.iota(jnp.int32, target_count)
    targets, target_labels = (
        lax.all_gather(own_targets, "row", axis=1, tiled=True),
        lax.all_gather(label_values, "row", axis=0, tiled=True),
    )
    target_index = position // tile * (n_col * tile) + col_at * tile + position % tile

    def hand_over(fates_now):
        incoming = shifted_2(fates_now, "pair", -1)
        return lax.all_gather(incoming, "row", axis=1, tiled=True)

    source_number = counts[pair_at]
    target_number = counts[pair_at + 1]
    source_total = source_number.astype(jnp.float32)
    target_total = target_number.astype(jnp.float32)
    source_index = row_at * source_count + lax.iota(jnp.int32, source_count)
    source_valid = source_index < source_number
    target_valid = target_index < target_number
    kernel = kernel_tile(sources, targets)
    start_terms = forward(kernel, target_valid.astype(jnp.float32)[None, :])[0]
    start_rows = lax.psum(start_terms, "col")
    source_mass = jnp.where(source_valid, source_growth / source_total, 0.0)
    scale_u = jnp.where(source_valid, jnp.power(source_mass / start_rows, source_power), 0.0)
    column_terms = backward(kernel, scale_u)
    column_totals = lax.psum(column_terms, "row")
    target_mass = target_valid.astype(jnp.float32) / target_total
    scale_v = jnp.where(target_valid, jnp.power(target_mass / column_totals, target_power), 0.0)
    own_offset = col_at * tile
    own_valid = lax.dynamic_slice_in_dim(source_valid, own_offset, tile, 0)
    own_scale = lax.dynamic_slice_in_dim(scale_u, own_offset, tile, 0)
    class_values = lax.iota(jnp.int32, CLASSES).astype(jnp.float32)
    label_table = jnp.where(
        (target_labels[None, :] == class_values[:, None]) & target_valid[None, :], 1.0, 0.0
    ).astype(jnp.float32)
    empty = jnp.zeros((CLASSES, tile), jnp.float32)
    final_terms = forward(kernel, scale_v[None, :])[0]
    final_rows = lax.psum(final_terms, "col")
    own_rows = lax.dynamic_slice_in_dim(final_rows, own_offset, tile, 0)
    safe_rows = jnp.where(own_valid, own_rows, 1.0)

    def advance(turn, fates_now):
        carried = jnp.where(is_last, label_table, hand_over(fates_now))
        terms = forward(kernel, carried * scale_v[None, :])
        sums = lax.psum_scatter(terms, "col", scatter_dimension=1, tiled=True)
        return jnp.where(own_valid[None, :], sums / safe_rows[None, :], 0.0)

    fates = lax.fori_loop(0, n_pair, advance, empty)
    mass = jnp.where(own_valid, source_total * own_scale * own_rows, 0.0)
    return (fates[None], mass[None])


LANES = 128
PIECES = 32
HALF = 16
BIG = 1e30
SCALE = 1.6986436005760381
MESH = pl.DeviceIdType.MESH


def split3(a):
    first = a.astype(jnp.bfloat16)
    rest = a - first.astype(jnp.float32)
    second = rest.astype(jnp.bfloat16)
    third = (rest - second.astype(jnp.float32)).astype(jnp.bfloat16)
    return first, second, third


def split2(a):
    first = a.astype(jnp.bfloat16)
    return first, (a - first.astype(jnp.float32)).astype(jnp.bfloat16)


def dot(a, b, dims):
    return lax.dot_general(a, b, (dims, ((), ())), preferred_element_type=jnp.float32)


def packed(block, extra):
    low = block[:HALF]
    rest = block.shape[0] - HALF
    fill = jnp.zeros((HALF - rest - 1, block.shape[1]), jnp.float32)
    high = jnp.concatenate([block[HALF:], extra, fill], axis=0)
    return jnp.concatenate([low, high], axis=1)


def unpacked(ref, start, stop):
    lows, highs = [], []
    lane = lax.broadcasted_iota(jnp.int32, (HALF, LANES), 1)
    for slot in range(start, stop, 2):
        a, b = ref[slot], ref[slot + 1]
        swap_a, swap_b = pltpu.roll(a, LANES // 2, 1), pltpu.roll(b, LANES // 2, 1)
        lows.append(jnp.where(lane < LANES // 2, a, swap_b))
        highs.append(jnp.where(lane < LANES // 2, swap_a, b))
    low, high = jnp.concatenate(lows, axis=1), jnp.concatenate(highs, axis=1)
    return jnp.concatenate([low, high], axis=0)


def fused(
    sizes,
    counts_in,
    coords_in,
    final_in,
    growth_in,
    labels_in,
    fates_ref,
    mass_ref,
    counts_ref,
    coords_ref,
    final_ref,
    growth_ref,
    labels_ref,
    xg,
    kernel,
    k1,
    k2,
    fin,
    fout,
    results,
    own_sems,
    x_send,
    x_recv,
    f_recv,
    result_recv,
    ready,
):
    n_pair, n_row, n_col, tile = sizes
    n_block = n_row * n_col
    near = n_block - n_row
    cells = n_block * tile
    pca = coords_in.shape[0]
    pair_at = lax.axis_index("pair")
    row_at = lax.axis_index("row")
    col_at = lax.axis_index("col")

    def place(slot):
        along, down = divmod(slot, n_row)
        return (row_at + down) % n_row, (col_at + along) % n_col

    barrier = pltpu.get_barrier_semaphore()
    mine = col_at * n_row + row_at

    def at(block):
        return block % n_row, block // n_row

    def signal(semaphore, pair, block):
        pl.semaphore_signal(
            semaphore, inc=1, device_id=(pair, *at(block)), device_id_type=MESH
        )

    def loop(start, stop, act):
        def step(block, carry):
            act(block)
            return carry

        lax.fori_loop(start, stop, step, 0)

    count_load = pltpu.make_async_copy(counts_in, counts_ref, own_sems.at[2])
    own_loads = (
        pltpu.make_async_copy(coords_in, coords_ref, own_sems.at[0]),
        pltpu.make_async_copy(growth_in, growth_ref, own_sems.at[1]),
        pltpu.make_async_copy(final_in, final_ref, f_recv),
        pltpu.make_async_copy(labels_in, labels_ref, result_recv),
    )
    for load in own_loads[:2]:
        load.start()

    def block_copy(time, pair, block):
        row, col = at(block)
        there = (col_at - col) % n_col * n_row + (row_at - row) % n_row
        return pltpu.make_async_remote_copy(
            src_ref=xg.at[time * n_block],
            dst_ref=xg.at[time * n_block + there],
            send_sem=x_send,
            recv_sem=x_recv.at[time - pair, there // near],
            device_id=(pair, row, col),
            device_id_type=MESH,
        )

    parts = ((0, near), (near, n_block))
    below = jnp.maximum(pair_at - 1, 0)

    def blocks(time, start, number):
        return xg.at[pl.ds(time * n_block + start, number)]

    def relay(time, part):
        start, stop = parts[part]
        block = blocks(time, start, stop - start)
        return pltpu.make_async_remote_copy(
            src_ref=block,
            dst_ref=block,
            send_sem=x_send,
            recv_sem=x_recv.at[time, part],
            device_id=(below, row_at, col_at),
            device_id_type=MESH,
        )

    f_copy = pltpu.make_async_remote_copy(
        src_ref=fout,
        dst_ref=fin,
        send_sem=x_send,
        recv_sem=f_recv,
        device_id=(below, row_at, col_at),
        device_id_type=MESH,
    )

    def arrival(buffer, sem):
        return pltpu.make_async_remote_copy(
            src_ref=buffer,
            dst_ref=buffer,
            send_sem=x_send,
            recv_sem=sem,
            device_id=(pair_at, row_at, col_at),
            device_id_type=MESH,
        )

    def inner(block):
        row, col = at(block)
        return (row > 0 and col > 0, -row - col, row)

    order = sorted(range(1, n_block), key=inner)

    def send(own, block):
        block_copy(own, min(own, 1), block).start()
        if own == 1:
            block_copy(n_pair, 1, block).start()

    def result_copy(pair):
        return pltpu.make_async_remote_copy(
            src_ref=results.at[pair],
            dst_ref=results.at[pair],
            send_sem=x_send,
            recv_sem=result_recv,
            device_id=(pair, row_at, col_at),
            device_id_type=MESH,
        )

    def only_send(first):
        for load in own_loads[:2]:
            load.wait()
        xg[first * n_block] = packed(coords_ref[:, 0, :], growth_ref[...])
        pl.semaphore_wait(barrier, 1)
        send(first, 0)
        pl.semaphore_wait(barrier, n_block - 1)
        for block in order:
            send(first, block)
        arrival(results.at[first], result_recv).wait_recv()
        fates_ref[0] = results[first, :CLASSES, :tile]
        mass_ref[...] = results[first, CLASSES : CLASSES + 1, :tile]
        arrival(blocks(0, 0, n_block), x_recv.at[0, 0]).wait_send()

    def body(first):
        odd = first == 1
        stop = n_pair if odd else 2
        loads = (*own_loads[: 4 if odd else 2], count_load)
        for load in loads[2:]:
            load.start()
        def allow():
            for block in (*order, 0):
                for pair in range(2, n_pair):
                    signal(barrier, pair, block)

        if odd:
            pl.when(mine == 0)(allow)
        else:
            signal(barrier, 1, mine)
        loop(mine + 1, n_block, functools.partial(signal, barrier, first))
        if odd:
            pl.semaphore_wait(barrier, mine + 1)
            pl.when(mine > 0)(allow)
        else:
            pl.when(mine > 0)(lambda: pl.semaphore_wait(barrier, mine))
        loop(0, mine, functools.partial(signal, ready, first))
        for load in loads[:-1]:
            load.wait()
        xg[first * n_block] = packed(coords_ref[:, 0, :], growth_ref[...])
        if odd:
            xg[n_pair * n_block] = packed(final_ref[...], labels_ref[...].astype(jnp.float32))
        pl.when(mine > 0)(lambda: send(first, 0))
        over = n_block - 1 - mine
        pl.when(over > 0)(lambda: pl.semaphore_wait(ready, over))
        for block in order:
            pl.when(mine != block)(functools.partial(send, first, block))
        count_load.wait()
        lane = lax.broadcasted_iota(jnp.int32, (1, LANES), 1)
        pieces = []
        for slot in range(0, n_block, 2):
            bases = []
            for one in (slot, slot + 1):
                row, col = place(one)
                bases.append((row * n_col + col) * tile)
            pieces.append(jnp.where(lane < tile, bases[0] + lane, bases[1] + lane - tile))
        index = jnp.concatenate(pieces, axis=1)
        valid = {time: index < counts_ref[time] for time in range(first, stop + 1)}
        numbers = {time: counts_ref[time].astype(jnp.float32) for time in range(first, stop + 1)}
        lefts, rights, extras, totals = {}, {}, {}, {}

        def arrive(part):
            for time in range(first, stop + 1):
                start, end = parts[part]
                if part == 0 and (time == first or (odd and time == n_pair)):
                    start = 1
                arrival(blocks(time, start, end - start), x_recv.at[time - first, part]).wait_recv()
                if odd and time < first + 2:
                    relay(time, part).start()

        def prepare(part):
            start, end = parts[part]
            width = (end - start) * tile
            lanes = slice(start * tile, end * tile)
            feature = lax.broadcasted_iota(jnp.int32, (PIECES, width), 0)
            for time in range(first, stop + 1):
                z = unpacked(xg, time * n_block + start, time * n_block + end)
                extras[time, part] = z[pca : pca + 1]
                z = jnp.where(feature < pca, z * SCALE, 0.0)
                norm = jnp.sum(z * z, axis=0, keepdims=True) * 0.5
                q = jnp.where(feature < pca, z, jnp.where(feature == pca, -norm, 1.0))
                q1, q2, q3 = split3(q)
                if time < stop:
                    rights[time, part] = jnp.concatenate([q1, q2, q1, q2, q3, q1], axis=0)
                if time > first:
                    low = jnp.where(valid[time][:, lanes], -norm, -BIG)
                    ends = jnp.where(feature[HALF:] == pca, 1.0, low)
                    pieces_of = [
                        jnp.concatenate(
                            [one[:HALF], jnp.where(feature[HALF:] < pca, one[HALF:], end)], axis=0
                        )
                        for one, end in zip((q1, q2, q3), split3(ends), strict=True)
                    ]
                    b1, b2, b3 = pieces_of
                    lefts[time, part] = jnp.concatenate([b1, b1, b2, b2, b1, b3], axis=0)

        def fill(pair, part, other):
            first_row, first_lane = parts[part][0] * tile, parts[other][0] * tile
            left, right = lefts[pair + 1, part], rights[pair, other]
            lanes = slice(first_lane, first_lane + right.shape[1])
            total = totals.get((pair, other), jnp.zeros((8, right.shape[1]), jnp.float32))
            for j in range(left.shape[1] // LANES):
                values = jnp.exp2(dot(left[:, j * LANES : (j + 1) * LANES], right, ((0,), (0,))))
                for k in range(LANES // 8):
                    total = total + values[k * 8 : (k + 1) * 8]
                rows = slice(first_row + j * LANES, first_row + (j + 1) * LANES)
                kernel[pair, rows, lanes] = values
            totals[pair, other] = total

        def extra(time):
            return jnp.concatenate([extras[time, 0], extras[time, 1]], axis=1)

        scale_u, row_totals = {}, {}
        iota_rows = lax.broadcasted_iota(jnp.int32, (tile, 1), 0)

        def settle(pairs):
            for pair in pairs:
                total = jnp.concatenate([totals[pair, 0], totals[pair, 1]], axis=1)
                total = jnp.sum(total, axis=0, keepdims=True)
                share = jnp.sqrt(extra(pair) / numbers[pair])
                scale_u[pair] = jnp.where(valid[pair], share * lax.rsqrt(total), 0.0)
            sums = {pair: jnp.zeros((8, cells), jnp.float32) for pair in pairs}
            for start in range(0, cells, 32):
                rows = slice(start, start + 32)
                row, col = place(start // tile)
                position = (row * n_col + col) * tile + start % tile + iota_rows[:32]
                for pair in pairs:
                    values = kernel[pair, rows, :]
                    terms = values * scale_u[pair]
                    folded = terms[:, :LANES]
                    for j in range(1, cells // LANES):
                        folded = folded + terms[:, j * LANES : (j + 1) * LANES]
                    column = jnp.sum(folded, axis=1, keepdims=True)
                    is_target = position < counts_ref[pair + 1]
                    column = jnp.where(is_target, column, 1.0)
                    power = jnp.log2(column) + jnp.log2(jnp.full((32, 1), numbers[pair + 1]))
                    scale_v = jnp.where(is_target, jnp.exp2(-target_power * power), 0.0)
                    scaled = values * scale_v
                    for k in range(32 // 8):
                        sums[pair] = sums[pair] + scaled[k * 8 : (k + 1) * 8]
                    high, low = split2(scaled)
                    k1[pair, rows, :] = high
                    k2[pair, rows, :] = low
            for pair in pairs:
                row_totals[pair] = jnp.sum(sums[pair], axis=0, keepdims=True)

        def moved(pair):
            mass = numbers[pair] * scale_u[pair] * row_totals[pair]
            return jnp.where(valid[pair], mass, 0.0)

        def advance(pair, fates):
            width = cells if pair > first else LANES
            share = jnp.where(valid[pair], 1.0 / row_totals[pair], 0.0)
            f1, f2 = split2(fates)
            high, low = k1[pair, :, :width], k2[pair, :, :width]
            if pair == n_pair - 1:
                sums = dot(f1, high, ((1,), (0,)))
            else:
                sums = dot(jnp.concatenate([f1, f2], axis=0), high, ((1,), (0,)))
                sums = sums[:CLASSES] + sums[CLASSES:]
            sums = sums + dot(f1, low, ((1,), (0,)))
            return sums * share[:, :width]

        lead = range(stop - 1, first if odd else first - 1, -1)
        arrive(0)
        prepare(0)
        for pair in lead:
            fill(pair, 0, 0)
        arrive(1)
        prepare(1)
        for pair in lead:
            fill(pair, 0, 1)
            fill(pair, 1, 0)
            fill(pair, 1, 1)
        settle(lead)
        share = {pair: jnp.where(valid[pair], 1.0 / row_totals[pair], 0.0) for pair in lead}
        if odd:
            classes = lax.broadcasted_iota(jnp.int32, (CLASSES, cells), 0).astype(jnp.float32)
            fates = jnp.where((extra(n_pair) == classes) & valid[n_pair], 1.0, 0.0)
        else:
            turned = jnp.transpose(jnp.broadcast_to(share[1], (8, cells)))[:, :1]
            near_high, near_low = k1[0, :, :LANES], k2[0, :, :LANES]
            scaled = (near_high.astype(jnp.float32) + near_low.astype(jnp.float32)) * turned
            b1, b2 = split2(scaled)
            both = dot(k1[1], jnp.concatenate([b1, b2], axis=1), ((1,), (0,)))
            chain = both[:, :LANES] + both[:, LANES:] + dot(k2[1], b1, ((1,), (0,)))
            h1, h2 = split2(chain)
            mass_ref[...] = moved(0)[:, :tile]
            arrival(blocks(0, 0, n_block - 1), x_recv.at[0, 0]).wait_send()
            f_copy.wait_recv()
            f1, f2 = split2(fin[...])
            both = dot(jnp.concatenate([f1, f2], axis=0), h1, ((1,), (0,)))
            both = both[:CLASSES] + both[CLASSES:] + dot(f1, h2, ((1,), (0,)))
            fates = both * share[0][:, :LANES]
        own = {}
        for pair in lead if odd else ():
            fates = advance(pair, fates)
            own[pair] = fates[:, :LANES]
        if odd:
            fout[...] = fates
            f_copy.start()
            for pair in lead:
                results[pair, :CLASSES] = own[pair]
                results[pair, CLASSES:] = jnp.broadcast_to(moved(pair)[:, :LANES], (8, LANES))
                result_copy(pair).start()
            for part in range(2):
                for other in range(2):
                    fill(first, part, other)
            settle([first])
            fates = advance(first, fates)
        fates_ref[0] = fates[:, :tile]
        if odd:
            mass_ref[...] = moved(first)[:, :tile]
            f_copy.wait_send()
            for pair in lead:
                result_copy(pair).wait_send()
            number = 2 * (n_block - 1) + 2 * n_block
            arrival(blocks(0, 0, number), x_recv.at[0, 0]).wait_send()

    for pair in range(n_pair):
        pl.when(pair_at == pair)(functools.partial(body if pair < 2 else only_send, pair))


def written(fates_ref, mass_ref, fates_out, mass_out, sems):
    copies = (
        pltpu.make_async_copy(mass_ref, mass_out, sems.at[0]),
        pltpu.make_async_copy(fates_ref, fates_out, sems.at[1]),
    )
    for copy in copies:
        copy.start()
    for copy in copies:
        copy.wait()


def per_device_fused(coords, final_coords, growth, counts, labels):
    pca, tile = coords.shape[1], coords.shape[2]
    n_pair = lax.axis_size("pair")
    n_row = lax.axis_size("row")
    n_col = lax.axis_size("col")
    n_block = n_row * n_col
    cells = n_block * tile
    vmem = pl.BlockSpec(memory_space=pltpu.VMEM)
    dma = pltpu.SemaphoreType.DMA
    fates, mass = pl.pallas_call(
        functools.partial(fused, (n_pair, n_row, n_col, tile)),
        out_shape=(
            pltpu.VMEM((1, CLASSES, tile), jnp.float32),
            pltpu.VMEM((1, tile), jnp.float32),
        ),
        in_specs=[pl.BlockSpec(memory_space=pl.ANY)] * 5,
        out_specs=(vmem, vmem),
        scratch_shapes=[
            pltpu.SMEM((n_pair + 1,), jnp.int32),
            pltpu.VMEM((pca, 1, tile), jnp.float32),
            pltpu.VMEM((pca, tile), jnp.float32),
            pltpu.VMEM((1, tile), jnp.float32),
            pltpu.VMEM((1, tile), jnp.int32),
            pltpu.VMEM(((n_pair + 1) * n_block, HALF, LANES), jnp.float32),
            pltpu.VMEM((n_pair, cells, cells), jnp.float32),
            pltpu.VMEM((n_pair, cells, cells), jnp.bfloat16),
            pltpu.VMEM((n_pair, cells, cells), jnp.bfloat16),
            pltpu.VMEM((CLASSES, cells), jnp.float32),
            pltpu.VMEM((CLASSES, cells), jnp.float32),
            pltpu.VMEM((n_pair, CLASSES + 8, LANES), jnp.float32),
            dma((3,)),
            dma,
            dma((n_pair, 2)),
            dma,
            dma,
            pltpu.SemaphoreType.REGULAR,
        ],
        compiler_params=pltpu.CompilerParams(collective_id=0, has_side_effects=True),
    )(counts, jnp.transpose(coords, (1, 0, 2)), final_coords, growth, labels[None, :])
    return pl.pallas_call(
        written,
        out_shape=(
            jax.ShapeDtypeStruct(fates.shape, jnp.float32),
            jax.ShapeDtypeStruct(mass.shape, jnp.float32),
        ),
        in_specs=(vmem, vmem),
        out_specs=(pl.BlockSpec(memory_space=pl.ANY), pl.BlockSpec(memory_space=pl.ANY)),
        scratch_shapes=[dma((2,))],
    )(*(pltpu.with_memory_space_constraint(array, pltpu.VMEM) for array in (fates, mass)))


def solution(mesh):
    placed = (
        P("pair", None, ("row", "col")),
        P(None, ("row", "col")),
        P("pair", ("row", "col")),
        P(),
        P(("row", "col")),
    )
    out = (P("pair", None, ("row", "col")), P("pair", ("row", "col")))

    def whole(coords, final_coords, growth, counts, labels):
        cells = coords.shape[2]
        pairs = mesh.shape["pair"]
        blocks = mesh.shape["row"] * mesh.shape["col"]
        fits = (
            2 * cells == LANES * blocks
            and mesh.shape["row"] % 2 == 0
            and mesh.shape["col"] > 1
            and pairs > 2
            and coords.shape[0] == pairs
            and coords.shape[1] + 2 <= PIECES
            and 8 * pairs * cells * cells <= FUSED_BYTES
        )
        body = per_device_fused if fits else per_device
        return jax.shard_map(
            body, mesh=mesh, in_specs=placed, out_specs=out, check_vma=False
        )(coords, final_coords, growth, counts, labels)

    return whole
```
